32 devices in a mesh: dp: 8 (over z, y), tp: 4 (over x, core).
Axes of the slice: x: 2, y: 2, z: 4, core: 2. Of those that a mesh axis runs over, the one named last changes fastest.
Arguments:
- frames: bfloat16 [16, 2304, 384], P('dp', 'tp'), may hold values from -6 to 6
- targets: bfloat16 [16, 2304, 384], P('dp', 'tp'), may hold values from -6 to 6
- presence: int32 [16, 4], P('dp'), may hold values 0 or 1
- order: int32 [8, 2], P('dp'), may hold values from 0 to 1, each once within a row
- attn_proj: float32 [3, 384, 384], P(None, None, 'tp'), may hold values from -0.3125 to 0.3125
- out_proj: float32 [384, 384], P('tp'), may hold values from -7 to 7
- up_proj: float32 [384, 1536], P(None, 'tp'), may hold values from -0.3125 to 0.3125
- up_bias: float32 [1536], P('tp'), may hold values from -3 to 3
- down_proj: float32 [384, 1536], P(None, 'tp'), may hold values from -0.15625 to 0.15625
- head_proj: float32 [384, 384], replicated, may hold values from -0.3125 to 0.3125
- vectors: float32 [9, 384], replicated
- momentum_attn: float32 [3, 384, 384], P(None, None, 'tp'), may hold values from -256 to 256
- momentum_out: float32 [384, 384], P('tp'), may hold values from -3 to 3
- momentum_up: float32 [384, 1536], P(None, 'tp'), may hold values from -3 to 3
- momentum_bias: float32 [1536], P('tp'), may hold values from -3 to 3
- momentum_down: float32 [384, 1536], P(None, 'tp'), may hold values from -3 to 3
- momentum_head: float32 [384, 384], replicated, may hold values from -224 to 224
- momentum_vectors: float32 [9, 384], replicated, may hold values from -3 to 3
- average_attn: float32 [3, 384, 384], P(None, None, 'tp'), may hold values from -0.3125 to 0.3125
- average_out: float32 [384, 384], P('tp'), may hold values from -7 to 7
- average_up: float32 [384, 1536], P(None, 'tp'), may hold values from -0.3125 to 0.3125
- average_bias: float32 [1536], P('tp'), may hold values from -3 to 3
- average_down: float32 [384, 1536], P(None, 'tp'), may hold values from -0.15625 to 0.15625
- average_head: float32 [384, 384], replicated, may hold values from -0.3125 to 0.3125
- average_vectors: float32 [9, 384], replicated
Outputs:
- loss: float32 [], replicated
- new_attn: float32 [3, 384, 384], P(None, None, 'tp')
- new_out: float32 [384, 384], P('tp')
- new_up: float32 [384, 1536], P(None, 'tp')
- new_bias: float32 [1536], P('tp')
- new_down: float32 [384, 1536], P(None, 'tp')
- new_head: float32 [384, 384], replicated
- new_vectors: float32 [9, 384], replicated
- moment_attn: float32 [3, 384, 384], P(None, None, 'tp')
- moment_out: float32 [384, 384], P('tp')
- moment_up: float32 [384, 1536], P(None, 'tp')
- moment_bias: float32 [1536], P('tp')
- moment_down: float32 [384, 1536], P(None, 'tp')
- moment_head: float32 [384, 384], replicated
- moment_vectors: float32 [9, 384], replicated
- mean_attn: float32 [3, 384, 384], P(None, None, 'tp')
- mean_out: float32 [384, 384], P('tp')
- mean_up: float32 [384, 1536], P(None, 'tp')
- mean_bias: float32 [1536], P('tp')
- mean_down: float32 [384, 1536], P(None, 'tp')
- mean_head: float32 [384, 384], replicated
- mean_vectors: float32 [9, 384], replicated
- grad_frames: float32 [16, 2304, 384], P('dp', 'tp')
The draws below stay inside these ranges and needn't reach their ends.
Inputs may be any that keep to these rules, and one draw needn't show every extreme that they name: `order`: each row holds every number below 2 once.
All inputs are finite; a program needn't handle non-finite values. No bound on the sum of `presence` on one device may be relied on, other than what follows from the above.
Results may differ from the reference program's by a relative error of at most 0.0095.
Values may be sent and summed in bfloat16 or wider, within the bound.
No kernel may reach another device: no remote copies, remote signals or barrier semaphores. Data moves between devices by JAX's collectives and lax.ppermute only.
A program may use at most 192 MiB of HBM per device.

```python
import jax
import jax.numpy as jnp
from jax import lax

D = 384
HEADS = 8
FF = 1536
STEMS = 4
CHN = 96
S = 2304
ITEM_DEV = 2
HDIM = 48
HEAD = 384
GROUPS = 8
ITEMS = 16


def vector_rows(key):
    base = jnp.clip(jax.random.normal(jax.random.fold_in(key, 11), (9, D), jnp.float32), -3.0, 3.0)
    spread = jax.random.uniform(jax.random.fold_in(key, 12), (9, D), jnp.float32, 0.5, 1.5)
    row_index = jnp.arange(9)[:, None]
    gain_rows = (row_index == 0) | (row_index == 4)
    scale_rows = (row_index == 3) | (row_index == 7)
    return jnp.where(gain_rows, 1.0 + 0.2 * base, jnp.where(scale_rows, spread, 0.3 * base))


def draw_vectors(key, part):
    return vector_rows(jax.random.fold_in(key, 3))


def draw_average_vectors(key, part):
    return vector_rows(jax.random.fold_in(key, 5))


def set_ends(values, own_key, low, top_value):
    shape = values.shape
    spot = [jax.random.randint(jax.random.fold_in(own_key, axis), (), 0, shape[axis]) for axis in range(len(shape))]
    values = values.at[tuple(spot)].set(low)
    longest = shape.index(max(shape))
    spot[longest] = (spot[longest] + 1) % shape[longest]
    return values.at[tuple(spot)].set(top_value)


def block_scale(rng, shape, shards, low, high):
    level = 1.0
    for position, shards_of in shards:
        steps = jax.random.uniform(jax.random.fold_in(jax.random.fold_in(rng, 6), position), (shards_of,), jnp.float32, low / len(shards), high / len(shards))
        level = level * jnp.repeat(jnp.exp(steps), shape[position] // shards_of).reshape((-1,) + (1,) * (len(shape) - 1 - position))
    return level


def scatter_about(key, shape, width, most, split=(), kind=jnp.bfloat16):
    values = jax.random.normal(key, shape, jnp.float32) * width
    if len(split) > 0:
        values = block_scale(key, shape, split, -0.22, 0.18) * values
    return jnp.clip(values, min=-most, max=most).astype(kind)


def setup_inputs(seed: int = 0) -> dict:
    seeds = jax.random.split(jax.random.key(seed), 26)
    return {
        "frames": scatter_about(seeds[0], (ITEMS, S, D), 1.0, 6.0, ((0, 8), (1, 4))),
        "targets": scatter_about(seeds[1], (ITEMS, S, HEAD), 1.0, 6.0, ((0, 8), (1, 4))),
        "presence": set_ends((jax.random.randint(seeds[2], (ITEMS, STEMS), 0, 4) < 3).astype(jnp.int32), jax.random.fold_in(seeds[2], 1), 0, 1),
        "order": jax.vmap(lambda own: jax.random.permutation(own, ITEM_DEV))(jax.random.split(seeds[3], GROUPS)).reshape((GROUPS, ITEM_DEV)).astype(jnp.int32),
        "attn_proj": scatter_about(seeds[4], (3, D, D), D ** -0.5, 0.3125, ((2, 4),), jnp.float32),
        "out_proj": scatter_about(seeds[5], (D, D), (S ** 0.5 / (2 * D ** 0.5)), 7.0, ((0, 4),), jnp.float32),
        "up_proj": scatter_about(seeds[6], (D, FF), D ** -0.5, 0.3125, ((1, 4),), jnp.float32),
        "up_bias": scatter_about(seeds[7], (FF,), 0.5, 3.0, ((0, 4),), jnp.float32),
        "down_proj": scatter_about(seeds[8], (D, FF), FF ** -0.5, 0.15625, ((1, 4),), jnp.float32),
        "head_proj": scatter_about(seeds[9], (D, HEAD), D ** -0.5, 0.3125, (), jnp.float32),
        "vectors": draw_vectors(jax.random.fold_in(seeds[25], 71), 0),
        "momentum_attn": scatter_about(seeds[11], (3, D, D), (0.5 * ITEMS * S / HEAD), 256.0, ((2, 4),), jnp.float32),
        "momentum_out": scatter_about(seeds[12], (D, D), ((ITEMS * S) ** 0.5 / HEAD), 3.0, ((0, 4),), jnp.float32),
        "momentum_up": scatter_about(seeds[13], (D, FF), ((ITEMS * S) ** 0.5 / HEAD), 3.0, ((1, 4),), jnp.float32),
        "momentum_bias": scatter_about(seeds[14], (FF,), ((ITEMS * S) ** 0.5 / HEAD), 3.0, ((0, 4),), jnp.float32),
        "momentum_down": scatter_about(seeds[15], (D, FF), ((ITEMS * S) ** 0.5 / HEAD), 3.0, ((1, 4),), jnp.float32),
        "momentum_head": scatter_about(seeds[16], (D, HEAD), (0.4 * ITEMS * S / HEAD), 224.0, (), jnp.float32),
        "momentum_vectors": scatter_about(seeds[17], (9, D), ((ITEMS * S) ** 0.5 / HEAD), 3.0, (), jnp.float32),
        "average_attn": scatter_about(seeds[18], (3, D, D), D ** -0.5, 0.3125, ((2, 4),), jnp.float32),
        "average_out": scatter_about(seeds[19], (D, D), (S ** 0.5 / (2 * D ** 0.5)), 7.0, ((0, 4),), jnp.float32),
        "average_up": scatter_about(seeds[20], (D, FF), D ** -0.5, 0.3125, ((1, 4),), jnp.float32),
        "average_bias": scatter_about(seeds[21], (FF,), 0.5, 3.0, ((0, 4),), jnp.float32),
        "average_down": scatter_about(seeds[22], (D, FF), FF ** -0.5, 0.15625, ((1, 4),), jnp.float32),
        "average_head": scatter_about(seeds[23], (D, HEAD), D ** -0.5, 0.3125, (), jnp.float32),
        "average_vectors": draw_average_vectors(jax.random.fold_in(seeds[25], 71), 0),
    }


@jax.custom_vjp
def low(v):
    return lax.optimization_barrier(v.astype(jnp.bfloat16)).astype(jnp.float32)

@jax.custom_vjp
def low_back(v):
    return v

def low_keep(v):
    return (low(v), None)

def low_pass(kept, grad):
    return (grad,)

def back_keep(v):
    return (v, None)

def back_low(kept, grad):
    return (low(grad),)
low.defvjp(low_keep, low_pass)
low_back.defvjp(back_keep, back_low)
EPSILON = 1e-05
MOMENTUM_RATE = 0.9
LEARN_RATE = 0.02
AVERAGE_RATE = 0.9
HIGH = lax.Precision.HIGHEST

def matmul(left, right):
    return jnp.dot(left, right, precision=HIGH)

def layer_norm(values, gain, shift):
    centred = values - lax.optimization_barrier(jnp.mean(values, axis=-1, keepdims=True))
    variance = lax.optimization_barrier(jnp.mean(centred * centred, axis=-1, keepdims=True))
    return centred * lax.rsqrt(variance + EPSILON) * gain + shift

def item_loss(params, frames, goal, keep):
    attn_proj, out_proj, up_proj, up_bias, down_proj, head_proj, vectors = params
    length = frames.shape[0]
    normed = low(layer_norm(frames, vectors[0], vectors[1]))
    query = low(low_back(matmul(normed, low(attn_proj[0])))).reshape(length, HEADS, HDIM)
    key_rows = low(low_back(matmul(normed, low(attn_proj[1])))).reshape(length, HEADS, HDIM)
    value_rows = low(low_back(matmul(normed, low(attn_proj[2])))).reshape(length, HEADS, HDIM)
    scores = low_back(jnp.einsum('qhd,khd->hqk', query, key_rows, precision=HIGH) * HDIM ** (-0.5))
    probs = low(jax.nn.softmax(scores, axis=-1))
    attended = low(low_back(jnp.einsum('hqk,khd->qhd', probs, value_rows, precision=HIGH))).reshape(length, D)
    middle = frames + vectors[3] * (low_back(matmul(attended, low(out_proj))) + vectors[2])
    second = low(layer_norm(middle, vectors[4], vectors[5]))
    hidden_pre = low_back(matmul(second, low(up_proj)) + up_bias)
    hidden = low(jax.nn.gelu(hidden_pre))
    final = middle + vectors[7] * (low_back(matmul(hidden, low(down_proj).T)) + vectors[6])
    pred = low_back(matmul(low(final), low(head_proj)) + vectors[8])
    diff = pred - goal
    return jnp.sum(keep * (jnp.sqrt(diff * diff + 1.0) - 1.0)) / HEAD

def update(weight, moment, average, grad):
    moment_new = MOMENTUM_RATE * moment + grad
    weight_new = weight - LEARN_RATE * (grad + MOMENTUM_RATE * moment_new)
    average_new = AVERAGE_RATE * average + (1.0 - AVERAGE_RATE) * weight_new
    return (weight_new, moment_new, average_new)

def reference(frames, targets, presence, order, attn_proj, out_proj, up_proj, up_bias, down_proj, head_proj, vectors, momentum_attn, momentum_out, momentum_up, momentum_bias, momentum_down, momentum_head, momentum_vectors, average_attn, average_out, average_up, average_bias, average_down, average_head, average_vectors):
    params = (attn_proj, out_proj, up_proj, up_bias, down_proj, head_proj, vectors)
    item_index = jnp.arange(ITEMS, dtype=jnp.int32)
    source = (item_index // ITEM_DEV * ITEM_DEV + order.reshape(-1)).astype(jnp.int32)
    keep_all = jnp.repeat(presence.astype(jnp.float32), CHN, axis=1)
    checked = jax.checkpoint(item_loss)
    frame_values = frames.astype(jnp.float32)

    def total(weights, frame_all):

        def step(carry, inputs):
            frame_rows, picked, keep = inputs
            goal = lax.dynamic_index_in_dim(targets, picked, 0, False).astype(jnp.float32)
            return (carry + checked(weights, frame_rows, goal, keep), None)
        summed, unused = lax.scan(step, jnp.zeros((), jnp.float32), (frame_all, source, keep_all))
        return summed
    loss, pull = jax.vjp(total, params, frame_values)
    grads, grad_frames = pull(jnp.ones((), jnp.float32))
    moments = (momentum_attn, momentum_out, momentum_up, momentum_bias, momentum_down, momentum_head, momentum_vectors)
    averages = (average_attn, average_out, average_up, average_bias, average_down, average_head, average_vectors)
    result = [update(params[place], moments[place], averages[place], grads[place]) for place in range(7)]
    return (loss, result[0][0], result[1][0], result[2][0], result[3][0], result[4][0], result[5][0], result[6][0], result[0][1], result[1][1], result[2][1], result[3][1], result[4][1], result[5][1], result[6][1], result[0][2], result[1][2], result[2][2], result[3][2], result[4][2], result[5][2], result[6][2], grad_frames)
```

```python
import math

import jax
import jax.numpy as jnp
from jax import lax
from jax.experimental import pallas as pl
from jax.experimental.pallas import tpu as pltpu
from jax.sharding import PartitionSpec as P

CHN = 96
HDIM = 48
HPAD = 64
HEAD = 384


EPSILON = 1e-05
MOMENTUM_RATE = 0.9
LEARN_RATE = 0.02
AVERAGE_RATE = 0.9
SCALE = HDIM ** (-0.5)
LOG_SCALE = SCALE * math.log2(math.e)
VMEM_LIMIT = 56 << 20

bf16 = jnp.bfloat16
f32 = jnp.float32


def contract(left, right, left_dim, right_dim):
    return lax.dot_general(
        left, right, (((left_dim,), (right_dim,)), ((), ())), preferred_element_type=f32
    )


def attention_forward_body(query, key, value, mixed, totals, weights):
    scores = contract(query[...], key[...], 0, 0)
    maximum = jnp.max(scores, axis=1, keepdims=True)
    exponent = jnp.exp2((scores - maximum) * LOG_SCALE).astype(bf16)
    weights[0] = exponent
    summed = contract(value[...], exponent, 1, 1)
    total = summed[HDIM : HDIM + 1]
    mixed[...] = (summed[:HDIM] / total).astype(bf16)
    totals[0] = total


def attention_forward(query, key, value):
    heads = query.shape[0] // HDIM
    rows, length = query.shape[1], key.shape[1]
    return pl.pallas_call(
        attention_forward_body,
        grid=(heads,),
        in_specs=[
            pl.BlockSpec((HDIM, rows), lambda h: (h, 0)),
            pl.BlockSpec((HDIM, length), lambda h: (h, 0)),
            pl.BlockSpec((HPAD, length), lambda h: (h, 0)),
        ],
        out_specs=[
            pl.BlockSpec((HDIM, rows), lambda h: (h, 0)),
            pl.BlockSpec((1, 1, rows), lambda h: (h, 0, 0)),
            pl.BlockSpec((1, rows, length), lambda h: (h, 0, 0)),
        ],
        out_shape=[
            jax.ShapeDtypeStruct((heads * HDIM, rows), bf16),
            jax.ShapeDtypeStruct((heads, 1, rows), f32),
            jax.ShapeDtypeStruct((heads, rows, length), bf16),
        ],
        compiler_params=pltpu.CompilerParams(vmem_limit_bytes=VMEM_LIMIT),
        cost_estimate=pl.CostEstimate(
            flops=heads * rows * length * 4 * 256,
            bytes_accessed=heads * rows * length * 2,
            transcendentals=heads * rows * length,
        ),
        name="attention_forward",
    )(query, key, value)


def attention_backward_body(
    query, key, value, mixed, grad_mixed, totals, weights, grad_query, grad_key, grad_value
):
    inverse = 1.0 / totals[0]
    grad = grad_mixed[...].astype(f32)
    delta = jnp.sum(grad * mixed[...].astype(f32), axis=0, keepdims=True)
    scaled = (grad * inverse).astype(bf16)
    offset = -delta * inverse
    high = offset.astype(bf16).astype(f32)
    low = offset - high
    row = lax.broadcasted_iota(jnp.int32, (HPAD - HDIM, offset.shape[1]), 0)
    extra = jnp.where(row == 0, high, jnp.where(row == 1, low, 0.0)).astype(bf16)
    grad_weights = contract(jnp.concatenate([scaled, extra], axis=0), value[...], 0, 0)
    kept = weights[0]
    grad_scores = (kept.astype(f32) * grad_weights).astype(bf16)
    grad_query[...] = (contract(key[...], grad_scores, 1, 1) * SCALE).astype(bf16)
    grad_key[...] = (contract(query[...], grad_scores, 1, 0) * SCALE).astype(bf16)
    grad_value[...] = contract(scaled, kept, 1, 0).astype(bf16)


def attention_backward(first, heads, query, key, value, mixed, grad_mixed, totals, weights):
    rows, length = query.shape[1], key.shape[1]
    rows_in = pl.BlockSpec((HDIM, rows), lambda h: (h + first, 0))
    rows_spec = pl.BlockSpec((HDIM, rows), lambda h: (h, 0))
    length_spec = pl.BlockSpec((HDIM, length), lambda h: (h, 0))
    return pl.pallas_call(
        attention_backward_body,
        grid=(heads,),
        in_specs=[
            rows_in,
            pl.BlockSpec((HDIM, length), lambda h: (h + first, 0)),
            pl.BlockSpec((HPAD, length), lambda h: (h + first, 0)),
            rows_in,
            rows_spec,
            pl.BlockSpec((1, 1, rows), lambda h: (h + first, 0, 0)),
            pl.BlockSpec((1, rows, length), lambda h: (h + first, 0, 0)),
        ],
        out_specs=[rows_spec, length_spec, length_spec],
        out_shape=[
            jax.ShapeDtypeStruct((heads * HDIM, rows), bf16),
            jax.ShapeDtypeStruct((heads * HDIM, length), bf16),
            jax.ShapeDtypeStruct((heads * HDIM, length), bf16),
        ],
        compiler_params=pltpu.CompilerParams(vmem_limit_bytes=VMEM_LIMIT),
        cost_estimate=pl.CostEstimate(
            flops=heads * rows * length * 8 * 256,
            bytes_accessed=heads * rows * length * 2,
            transcendentals=0,
        ),
        name="attention_backward",
    )(query, key, value, mixed, grad_mixed, totals, weights)


GELU_A = math.sqrt(2.0 / math.pi)
GELU_B = 0.044715
SMALL = 16
BLOCK = 384


def split_small(values):
    high = values.astype(bf16)
    return high, (values - high.astype(f32)).astype(bf16)


def row_mean(values):
    return jnp.mean(values, axis=-1, keepdims=True)


def column_sum(values):
    return jnp.sum(values, axis=0, keepdims=True)


def middle_body(
    place,
    attended,
    frames,
    goal,
    keep,
    vectors,
    bias,
    out_low,
    up_low,
    down_low,
    head_low,
    grad_middle_out,
    grad_attended_out,
    kept_out,
    sent_out,
    sum_out,
    sum_up,
    sum_down,
    sum_head,
    sum_small,
    sum_bias,
):
    step = pl.program_id(0)

    @pl.when(step == 0)
    def _():
        for total in (sum_out, sum_up, sum_down, sum_head, sum_small, sum_bias):
            total[...] = jnp.zeros_like(total)

    gain, shift = vectors[4:5], vectors[5:6]
    scale_one, scale_two = vectors[3:4], vectors[7:8]
    biased_one = contract(attended[...], out_low[...], 0, 0) + vectors[2:3]
    middle = frames[...].astype(f32) + scale_one * biased_one
    centred = middle - row_mean(middle)
    inverse = lax.rsqrt(row_mean(centred * centred) + EPSILON)
    normed = centred * inverse
    second = (normed * gain + shift).astype(bf16)
    pre = contract(second, up_low[...], 1, 0) + bias[...]
    square = pre * pre
    tanh = jnp.tanh(GELU_A * (pre + GELU_B * square * pre))
    phi = 0.5 * (1.0 + tanh)
    hidden = (pre * phi).astype(bf16)
    slope = phi + pre * (0.5 * GELU_A) * (1.0 - tanh * tanh) * (1.0 + 3.0 * GELU_B * square)
    biased_two = contract(hidden, down_low[...], 1, 1) + vectors[6:7]
    final = middle + scale_two * biased_two
    final_low = final.astype(bf16)
    pred = contract(final_low, head_low[...], 1, 0) + vectors[8:9]
    diff = pred - goal[...].astype(f32)
    smooth = jnp.sqrt(diff * diff + 1.0)
    loss = column_sum(keep[...] * (smooth - 1.0)) / HEAD
    grad_pred = (keep[...] * (diff / smooth) / HEAD).astype(bf16)
    sum_head[...] += contract(final_low, grad_pred, 0, 0)
    grad_final = contract(grad_pred, head_low[...], 1, 1)
    grad_ffn = grad_final * scale_two
    ffn_low = grad_ffn.astype(bf16)
    grad_hidden = contract(ffn_low, down_low[...], 1, 0)
    sum_down[...] += contract(ffn_low, hidden, 0, 0)
    grad_pre = grad_hidden * slope
    pre_low = grad_pre.astype(bf16)
    sum_up[...] += contract(second, pre_low, 0, 0)
    sum_bias[...] += column_sum(pre_low.astype(f32))
    grad_second = contract(pre_low, up_low[...], 1, 1)
    scaled = grad_second * gain
    back = inverse * (scaled - row_mean(scaled) - normed * row_mean(scaled * normed))
    grad_middle = grad_final + back
    grad_attn = grad_middle * scale_one
    attn_low = grad_attn.astype(bf16)
    sum_out[...] += contract(attended[...], attn_low, 1, 0)
    grad_attended_out[...] = contract(out_low[...], attn_low, 1, 1).astype(bf16)
    grad_middle_out[...] = grad_middle
    rows = [
        column_sum(grad_attn),
        column_sum(grad_middle * biased_one),
        column_sum(grad_second * normed),
        column_sum(grad_second),
        column_sum(grad_ffn),
        column_sum(grad_final * biased_two),
        column_sum(grad_pred.astype(f32)),
        loss,
    ]
    sum_small[0:8] += jnp.concatenate(rows, axis=0)

    @pl.when(step == pl.num_programs(0) - 1)
    def _():
        share = sum_out.shape[0] // 4
        deep, width = sum_up.shape[0], sum_up.shape[1] // 4
        count = share + 2 * deep
        half = sum_head.shape[0] // 2
        core = lax.rem(place[0], 2)
        for j in range(4):
            target = (kept_out, sent_out)[j % 2]
            base = (j // 2) * count
            columns = slice(j * width, (j + 1) * width)
            target[base : base + share] = sum_out[j * share : (j + 1) * share].astype(bf16)
            target[base + share : base + share + deep] = sum_up[:, columns].astype(bf16)
            target[base + share + deep : base + count] = sum_down[:, columns].astype(bf16)
            sum_small[pl.ds(8 + lax.bitwise_xor(place[0], j), 1)] = sum_bias[:, columns]
        base = 2 * count
        kept_out[base : base + half] = sum_head[pl.ds(pl.multiple_of(core * half, half), half)].astype(bf16)
        sent_out[base : base + half] = sum_head[
            pl.ds(pl.multiple_of((1 - core) * half, half), half)
        ].astype(bf16)
        column = lax.broadcasted_iota(jnp.int32, (1, HEAD), 1)
        total = jnp.sum(sum_small[7:8], axis=1, keepdims=True)
        sum_small[7:8] = jnp.where(column == 0, total, 0.0)
        high, low = split_small(sum_small[...])
        for target in (kept_out, sent_out):
            target[base + half : base + half + SMALL] = high
            target[base + half + SMALL : base + half + 2 * SMALL] = low


def middle_step(
    place, attended, frames, goal, keep, vectors, bias, out_low, up_low, down_low, head_low
):
    rows, model = frames.shape
    share, wide = out_low.shape[0] // 4, up_low.shape[1]
    count = 2 * (share + 2 * model) + HEAD // 2 + 2 * SMALL

    def whole(array):
        return pl.BlockSpec(array.shape, lambda i, place: (0, 0))

    by_row = pl.BlockSpec((BLOCK, model), lambda i, place: (i, 0))
    by_column = pl.BlockSpec((model, BLOCK), lambda i, place: (0, i))
    payload = pl.BlockSpec((count, HEAD), lambda i, place: (0, 0))
    fixed = (keep, vectors, bias, out_low, up_low, down_low, head_low)
    return pl.pallas_call(
        middle_body,
        grid_spec=pltpu.PrefetchScalarGridSpec(
            num_scalar_prefetch=1,
            grid=(rows // BLOCK,),
            in_specs=[by_column, by_row, by_row] + [whole(a) for a in fixed],
            out_specs=[by_row, by_column, payload, payload],
            scratch_shapes=[
                pltpu.VMEM(out_low.shape, f32),
                pltpu.VMEM(up_low.shape, f32),
                pltpu.VMEM(down_low.shape, f32),
                pltpu.VMEM(head_low.shape, f32),
                pltpu.VMEM((SMALL, HEAD), f32),
                pltpu.VMEM((1, wide), f32),
            ],
        ),
        out_shape=[
            jax.ShapeDtypeStruct((rows, model), f32),
            jax.ShapeDtypeStruct((model, rows), bf16),
            jax.ShapeDtypeStruct((count, HEAD), bf16),
            jax.ShapeDtypeStruct((count, HEAD), bf16),
        ],
        compiler_params=pltpu.CompilerParams(vmem_limit_bytes=VMEM_LIMIT),
        cost_estimate=pl.CostEstimate(
            flops=rows * model * (12 * wide + 12 * model),
            bytes_accessed=10 * model * wide,
            transcendentals=rows * wide,
        ),
        name="middle_step",
    )(place, attended, frames, goal, *fixed)


def add_small(left, right, start):
    ends = [(r[start : start + SMALL].astype(f32), r[start + SMALL :].astype(f32)) for r in (left, right)]
    return (ends[0][0] + ends[0][1]) + (ends[1][0] + ends[1][1])


def add_rows(left, right, start, stop):
    return left[start:stop].astype(f32) + right[start:stop].astype(f32)


def fold_core_body(block, left, right, kept, sent):
    small = left.shape[0] - 2 * SMALL
    kept[:block] = add_rows(left, right, 0, block).astype(bf16)
    sent[:block] = add_rows(left, right, block, 2 * block).astype(bf16)
    shared = small - 2 * block
    high, low = split_small(add_small(left, right, small))
    for target in (kept, sent):
        if shared:
            target[block : block + shared] = add_rows(left, right, 2 * block, small).astype(bf16)
        target[block + shared : block + shared + SMALL] = high
        target[block + shared + SMALL :] = low


def fold_core(block, left, right):
    shape = jax.ShapeDtypeStruct((left.shape[0] - block, left.shape[1]), bf16)
    return pl.pallas_call(
        lambda *refs: fold_core_body(block, *refs),
        out_shape=[shape, shape],
        compiler_params=pltpu.CompilerParams(vmem_limit_bytes=VMEM_LIMIT),
        cost_estimate=pl.CostEstimate(flops=left.size, bytes_accessed=8 * left.size, transcendentals=0),
        name="fold_core",
    )(left, right)


def fold_body(left, right, total):
    small = left.shape[0] - 2 * SMALL
    both = add_small(left, right, small)
    total[:small] = add_rows(left, right, 0, small).astype(total.dtype)
    if total.dtype == f32:
        total[small:] = both
    else:
        high, low = split_small(both)
        total[small : small + SMALL] = high
        total[small + SMALL :] = low


def fold(left, right, last=False):
    rows = left.shape[0]
    shape = jax.ShapeDtypeStruct((rows - SMALL, left.shape[1]), f32) if last else left
    return pl.pallas_call(
        fold_body,
        out_shape=jax.ShapeDtypeStruct(shape.shape, shape.dtype),
        compiler_params=pltpu.CompilerParams(vmem_limit_bytes=VMEM_LIMIT),
        cost_estimate=pl.CostEstimate(flops=left.size, bytes_accessed=6 * left.size, transcendentals=0),
        name="fold",
    )(left, right)


def product(left, right, form):
    return jnp.einsum(form, left, right, preferred_element_type=jnp.float32)


def norm_forward(values, gain, shift):
    centred = values - jnp.mean(values, axis=-1, keepdims=True)
    inverse = lax.rsqrt(jnp.mean(centred * centred, axis=-1, keepdims=True) + EPSILON)
    normed = centred * inverse
    return (normed * gain + shift, normed, inverse)


def norm_backward(grad, normed, inverse, gain):
    scaled = grad * gain
    back = inverse * (
        scaled
        - jnp.mean(scaled, axis=-1, keepdims=True)
        - normed * jnp.mean(scaled * normed, axis=-1, keepdims=True)
    )
    return (back, jnp.sum(grad * normed, axis=0), jnp.sum(grad, axis=0))


def update(weight, moment, average, grad):
    moment_new = MOMENTUM_RATE * moment + grad
    weight_new = weight - LEARN_RATE * (grad + MOMENTUM_RATE * moment_new)
    average_new = AVERAGE_RATE * average + (1.0 - AVERAGE_RATE) * weight_new
    return (weight_new, moment_new, average_new)


CORE_PAIRS = [(0, 1), (1, 0), (2, 3), (3, 2)]
CHIP_PAIRS = [(0, 2), (2, 0), (1, 3), (3, 1)]


def swap_core(values):
    return lax.ppermute(values, "tp", CORE_PAIRS)


def swap_chip(values):
    return lax.ppermute(values, "tp", CHIP_PAIRS)


def swap_dp(values, step, size):
    return lax.ppermute(values, "dp", [(i, i ^ step) for i in range(size)])


def pick(stacked, place):
    return lax.dynamic_index_in_dim(stacked, place, 0, False)


def rounded(values):
    return lax.reduce_precision(values, 8, 7)


def two_part(values):
    high = rounded(values)
    return jnp.concatenate([high, rounded(values - high)], axis=0)


def per_device(
    frames,
    targets,
    presence,
    order,
    attn_proj,
    out_proj,
    up_proj,
    up_bias,
    down_proj,
    head_proj,
    vectors,
    momentum_attn,
    momentum_out,
    momentum_up,
    momentum_bias,
    momentum_down,
    momentum_head,
    momentum_vectors,
    average_attn,
    average_out,
    average_up,
    average_bias,
    average_down,
    average_head,
    average_vectors,
):
    size = lax.axis_size("dp")
    place = lax.axis_index("tp")
    chip, core = place // 2, place % 2
    width = up_proj.shape[1]
    own = pick(frames, chip)
    got = swap_chip(pick(frames, 1 - chip))
    mine = jnp.concatenate([own, got], axis=0)
    rows = mine.shape[0]
    theirs = swap_core(mine)
    every = jnp.concatenate([mine, theirs], axis=0)
    attn_own = jnp.swapaxes(attn_proj, 1, 2).astype(bf16)
    attn_core = swap_core(attn_own)
    attn_chip = swap_chip(attn_own)
    attn_both = swap_core(attn_chip)
    near = jnp.concatenate([attn_own, attn_core], axis=1)
    far = jnp.concatenate([attn_chip, attn_both], axis=1)
    rest = jnp.concatenate([out_proj, up_proj, down_proj], axis=0).astype(bf16)
    sent = jnp.concatenate([rest, pick(targets, order[0, 1 - chip])], axis=0)
    got_sent = swap_chip(sent)
    rest_rows = rest.shape[0]
    rest_core = swap_core(rest)
    rest_chip = got_sent[:rest_rows]
    rest_both = swap_core(rest_chip)
    blocks = [rest, rest_core, rest_chip, rest_both]
    share = out_proj.shape[0]
    deep = up_proj.shape[0]
    out_all = jnp.concatenate([b[:share] for b in blocks], axis=0)
    up_all = jnp.concatenate([b[share : share + deep] for b in blocks], axis=1)
    down_all = jnp.concatenate([b[share + deep :] for b in blocks], axis=1)
    bias_core = swap_core(up_bias)
    bias_chip = swap_chip(up_bias)
    bias_all = jnp.concatenate([up_bias, bias_core, bias_chip, swap_core(bias_chip)])
    goal = jnp.concatenate([pick(targets, order[0, chip]), got_sent[rest_rows:]], axis=0)
    keep = jnp.repeat(pick(presence, chip).astype(f32), CHN)[None, :]
    head_low = head_proj.astype(bf16)

    first, hat_all, inv_all = norm_forward(every.astype(f32), vectors[0], vectors[1])
    first_low = first.astype(bf16)
    start = mine.astype(f32)
    hat_one, inv_one = hat_all[:rows], inv_all[:rows]

    def project(block):
        query = product(block[0], first_low[:rows], "ed,nd->en").astype(bf16)
        key = product(block[1], first_low, "ed,nd->en").astype(bf16)
        value = product(block[2], first_low, "ed,nd->en").astype(bf16)
        heads = value.shape[0] // HDIM
        length = value.shape[1]
        ones = jnp.ones((heads, 2, length), bf16)
        zeros = jnp.zeros((heads, HPAD - HDIM - 2, length), bf16)
        value = jnp.concatenate([value.reshape(heads, HDIM, length), ones, zeros], axis=1)
        return query, key, value.reshape(heads * HPAD, length)

    inputs = [project(block) for block in (near, far)]
    outputs = [attention_forward(*part) for part in inputs]
    attended = jnp.concatenate([part[0] for part in outputs], axis=0)
    grad_middle, grad_attended, kept, sent = middle_step(
        place.reshape(1), attended, mine, goal, keep, vectors, bias_all[None], out_all, up_all, down_all, head_low
    )

    per_block = share // HDIM
    grads = [None] * 4

    def backward(j, after):
        part, output = inputs[j // 2], outputs[j // 2]
        grad = grad_attended[j * share : (j + 1) * share]
        if after is not None:
            grad, after = lax.optimization_barrier((grad, after))
        grads[j] = attention_backward(
            (j % 2) * per_block, per_block, *part, output[0], grad, output[1], output[2]
        )
        return after

    block_rows = share + 2 * deep
    got_core = swap_core(sent)
    kept, sent = fold_core(block_rows, kept, got_core)
    kept = backward(2, kept)
    got_chip = swap_chip(sent)
    backward(3, None)
    kept = fold(kept, got_chip)
    kept = backward(1, kept)
    steps = [1 << k for k in range(size.bit_length() - 1)]
    got = swap_dp(kept, steps[0], size)
    backward(0, None)
    kept = fold(kept, got, last=len(steps) == 1)
    for step in steps[1:]:
        kept = fold(kept, swap_dp(kept, step, size), last=step == steps[-1])
    grad_out = kept[:share]
    grad_up = kept[share : share + deep]
    grad_down = kept[share + deep : block_rows]
    half = HEAD // 2
    head_mine = kept[block_rows : block_rows + half]
    head_other = swap_core(head_mine)
    grad_head = jnp.where(
        core == 0,
        jnp.concatenate([head_mine, head_other], axis=0),
        jnp.concatenate([head_other, head_mine], axis=0),
    )
    small = kept[block_rows + half :]
    loss = small[7, 0]
    grad_up_bias = pick(small[8:12], place)

    all_weights = jnp.concatenate([near, far], axis=1)
    grad_query, grad_key, grad_value = (
        jnp.concatenate([g[k] for g in grads], axis=0) for k in range(3)
    )
    pulled = product(grad_key, all_weights[1], "en,ed->nd") + product(grad_value, all_weights[2], "en,ed->nd")
    query_part = product(grad_query, all_weights[0], "en,ed->nd")
    grad_attn_proj = jnp.stack(
        [
            product(grad_query, first_low[:rows], "en,nd->ed"),
            product(grad_key, first_low, "en,nd->ed"),
            product(grad_value, first_low, "en,nd->ed"),
        ]
    ).reshape(3, 4, share, HEAD)
    other_rows = swap_core(pulled[rows:].astype(bf16)).astype(f32)
    grad_one = pulled[:rows] + query_part + other_rows
    back_one, grad_gain_one, grad_shift_one = norm_backward(grad_one, hat_one, inv_one, vectors[0])
    grad_rows = grad_middle + back_one
    quarter = rows // 2
    returned = swap_chip(grad_rows[quarter:].astype(bf16)).astype(f32)
    grad_frames = jnp.where(
        chip == 0,
        jnp.stack([grad_rows[:quarter], returned]),
        jnp.stack([returned, grad_rows[:quarter]]),
    )
    zeros = jnp.zeros((SMALL - 2, HEAD), f32)
    parts = two_part(jnp.concatenate([grad_gain_one[None], grad_shift_one[None], zeros], axis=0))
    blocks = [grad_attn_proj[:, j].reshape(3 * share, HEAD) for j in range(4)]
    kept = jnp.concatenate([blocks[0], blocks[2], parts], axis=0).astype(bf16)
    sent = jnp.concatenate([blocks[1], blocks[3], parts], axis=0).astype(bf16)
    kept, sent = fold_core(3 * share, kept, swap_core(sent))
    kept = fold(kept, swap_chip(sent))
    for step in steps:
        kept = fold(kept, swap_dp(kept, step, size), last=step == steps[-1])
    grad_attn_proj = jnp.swapaxes(kept[: 3 * share].reshape(3, share, HEAD), 1, 2)
    grad_vectors = jnp.concatenate([kept[3 * share : 3 * share + 2], small[:7]], axis=0)
    first_set = update(attn_proj, momentum_attn, average_attn, grad_attn_proj)
    second_set = update(out_proj, momentum_out, average_out, grad_out)
    third_set = update(up_proj, momentum_up, average_up, grad_up)
    fourth_set = update(up_bias, momentum_bias, average_bias, grad_up_bias)
    fifth_set = update(down_proj, momentum_down, average_down, grad_down)
    sixth_set = update(head_proj, momentum_head, average_head, grad_head)
    seventh_set = update(vectors, momentum_vectors, average_vectors, grad_vectors)
    return (
        loss,
        first_set[0],
        second_set[0],
        third_set[0],
        fourth_set[0],
        fifth_set[0],
        sixth_set[0],
        seventh_set[0],
        first_set[1],
        second_set[1],
        third_set[1],
        fourth_set[1],
        fifth_set[1],
        sixth_set[1],
        seventh_set[1],
        first_set[2],
        second_set[2],
        third_set[2],
        fourth_set[2],
        fifth_set[2],
        sixth_set[2],
        seventh_set[2],
        grad_frames,
    )


def solution(mesh):
    in_specs = (
        P("dp", "tp", None),
        P("dp", "tp", None),
        P("dp", None),
        P("dp", None),
        P(None, None, "tp"),
        P("tp", None),
        P(None, "tp"),
        P("tp"),
        P(None, "tp"),
        P(),
        P(),
        P(None, None, "tp"),
        P("tp", None),
        P(None, "tp"),
        P("tp"),
        P(None, "tp"),
        P(),
        P(),
        P(None, None, "tp"),
        P("tp", None),
        P(None, "tp"),
        P("tp"),
        P(None, "tp"),
        P(),
        P(),
    )
    out_specs = (
        P(),
        P(None, None, "tp"),
        P("tp", None),
        P(None, "tp"),
        P("tp"),
        P(None, "tp"),
        P(),
        P(),
        P(None, None, "tp"),
        P("tp", None),
        P(None, "tp"),
        P("tp"),
        P(None, "tp"),
        P(),
        P(),
        P(None, None, "tp"),
        P("tp", None),
        P(None, "tp"),
        P("tp"),
        P(None, "tp"),
        P(),
        P(),
        P("dp", "tp", None),
    )
    return jax.shard_map(
        per_device, mesh=mesh, in_specs=in_specs, out_specs=out_specs, check_vma=False
    )
```

```python
import functools
import math

import jax
import jax.numpy as jnp
from jax import lax
from jax.experimental import pallas as pl
from jax.experimental.pallas import tpu as pltpu
from jax.sharding import PartitionSpec as P

CHN = 96
HDIM = 48
HPAD = 64
HEAD = 384


EPSILON = 1e-05
MOMENTUM_RATE = 0.9
LEARN_RATE = 0.02
AVERAGE_RATE = 0.9
SCALE = HDIM ** (-0.5)
LOG_SCALE = SCALE * math.log2(math.e)
GELU_A = math.sqrt(2.0 / math.pi)
GELU_B = 0.044715
SMALL = 16
BLOCK = 384
ROWS = 64

bf16 = jnp.bfloat16
f32 = jnp.float32
HBM = pl.BlockSpec(memory_space=pltpu.HBM)
SMEM = pl.BlockSpec(memory_space=pltpu.SMEM)
VMEM = pl.BlockSpec(memory_space=pltpu.VMEM)


def kernel_call(body, outs, inputs, limit, micros, name, in_specs=None, out_specs=None, scratch=(), aliases=None):
    return pl.pallas_call(
        body,
        out_shape=outs,
        in_specs=in_specs or [VMEM] * len(inputs),
        out_specs=out_specs or jax.tree.map(lambda _: VMEM, outs),
        scratch_shapes=list(scratch),
        input_output_aliases=aliases or {},
        compiler_params=pltpu.CompilerParams(vmem_limit_bytes=limit << 20),
        cost_estimate=pl.CostEstimate(flops=int(micros * 1e9), bytes_accessed=0, transcendentals=0),
        name=name,
    )(*inputs)


def struct(rows, columns, dtype):
    return jax.ShapeDtypeStruct((rows, columns), dtype)


def contract(left, right, left_dim, right_dim):
    return lax.dot_general(
        left, right, (((left_dim,), (right_dim,)), ((), ())), preferred_element_type=f32
    )


def row_mean(values):
    return jnp.mean(values, axis=-1, keepdims=True)


def column_sum(values):
    return jnp.sum(values, axis=0, keepdims=True)


def normalise(values):
    centred = values - row_mean(values)
    inverse = lax.rsqrt(row_mean(centred * centred) + EPSILON)
    return centred * inverse, inverse


def aligned(index, size):
    return pl.ds(pl.multiple_of(index * size, size), size)


def forward_body(first, heads, query, key, value, *refs):
    mixed, totals, weights, slots, sems = refs[-5:]

    def out_copy(h):
        slot = lax.rem(h, 2)
        return pltpu.make_async_copy(slots.at[slot], weights.at[h + first], sems.at[slot])

    def head(h, carry):
        @pl.when(h >= 2)
        def _():
            out_copy(h - 2).wait()

        rows = aligned(h, HDIM)
        scores = contract(query[rows], key[rows], 0, 0)
        maximum = jnp.max(scores, axis=1, keepdims=True)
        exponent = jnp.exp2((scores - maximum) * LOG_SCALE).astype(bf16)
        slots[lax.rem(h, 2)] = exponent
        out_copy(h).start()
        summed = contract(value[aligned(h, HPAD)], exponent, 1, 1)
        total = summed[HDIM : HDIM + 1]
        mixed[rows] = (summed[:HDIM] / total).astype(bf16)
        totals[pl.ds(h, 1)] = total
        return carry

    lax.fori_loop(0, heads, head, 0)
    for h in range(max(0, heads - 2), heads):
        out_copy(h).wait()


def attention_forward(query, key, value, weights=None):
    heads = query.shape[0] // HDIM
    first = 0 if weights is None else heads
    rows, length = query.shape[1], key.shape[1]
    return kernel_call(
        functools.partial(forward_body, first, heads),
        [
            struct(heads * HDIM, rows, bf16),
            struct(heads, rows, f32),
            jax.ShapeDtypeStruct((2 * heads, rows, length), bf16),
        ],
        (query, key, value) if weights is None else (query, key, value, weights),
        FORWARD_LIMIT,
        4 * heads,
        "attention_forward",
        in_specs=[VMEM] * 3 if weights is None else [VMEM] * 3 + [HBM],
        aliases={} if weights is None else {3: 2},
        out_specs=[VMEM, VMEM, HBM],
        scratch=[pltpu.VMEM((2, rows, length), bf16), pltpu.SemaphoreType.DMA((2,))],
    )


def backward_body(
    first, base, heads, query, key, value, mixed, grad_mixed, totals, weights,
    grad_query, grad_key, grad_value, slots, sems
):
    def in_copy(h):
        slot = lax.rem(h, 2)
        return pltpu.make_async_copy(weights.at[h + base], slots.at[slot], sems.at[slot])

    in_copy(0).start()

    def head(h, carry):
        @pl.when(h + 1 < heads)
        def _():
            in_copy(h + 1).start()

        rows, here = aligned(h + first, HDIM), aligned(h, HDIM)
        inverse = 1.0 / totals[pl.ds(h + first, 1)]
        grad = grad_mixed[rows].astype(f32)
        delta = column_sum(grad * mixed[rows].astype(f32))
        scaled = (grad * inverse).astype(bf16)
        offset = -delta * inverse
        high = offset.astype(bf16).astype(f32)
        row = lax.broadcasted_iota(jnp.int32, (HPAD - HDIM, offset.shape[1]), 0)
        extra = jnp.where(row == 0, high, jnp.where(row == 1, offset - high, 0.0)).astype(bf16)
        grad_weights = contract(
            jnp.concatenate([scaled, extra], axis=0), value[aligned(h + first, HPAD)], 0, 0
        )
        in_copy(h).wait()
        kept = slots[lax.rem(h, 2)]
        grad_scores = (kept.astype(f32) * grad_weights).astype(bf16)
        grad_query[here] = (contract(key[rows], grad_scores, 1, 1) * SCALE).astype(bf16)
        grad_key[here] = (contract(query[rows], grad_scores, 1, 0) * SCALE).astype(bf16)
        grad_value[here] = contract(scaled, kept, 1, 0).astype(bf16)
        return carry

    lax.fori_loop(0, heads, head, 0)


def attention_backward(first, base, heads, query, key, value, mixed, grad_mixed, totals, weights):
    rows, length = query.shape[1], key.shape[1]
    return kernel_call(
        functools.partial(backward_body, first, base, heads),
        [
            struct(heads * HDIM, rows, bf16),
            struct(heads * HDIM, length, bf16),
            struct(heads * HDIM, length, bf16),
        ],
        (query, key, value, mixed, grad_mixed, totals, weights),
        BACKWARD_LIMIT,
        5.5 * heads,
        "attention_backward",
        in_specs=[VMEM] * 6 + [HBM],
        scratch=[pltpu.VMEM((2, rows, length), bf16), pltpu.SemaphoreType.DMA((2,))],
    )


def take_body(place, stacked, taken):
    taken[...] = stacked[place[0]]


def take(stacked, place):
    count, rows, columns = stacked.shape
    return kernel_call(
        take_body, struct(rows, columns, stacked.dtype), (place, stacked), 2, 1, "take", in_specs=[SMEM, VMEM]
    )


def pack_body(place, attn, out, up, down, bias, targets, attn_low, sent, goal):
    share, deep = out.shape[0], up.shape[0]
    base = share + 2 * deep
    goal[...] = targets[place[0]]
    attn_low[...] = attn[...].astype(bf16)
    sent[:share] = out[...].astype(bf16)
    sent[share : share + deep] = up[...].astype(bf16)
    sent[share + deep : base] = down[...].astype(bf16)
    high = bias[...].astype(bf16)
    low = (bias[...] - high.astype(f32)).astype(bf16)
    zeros = jnp.zeros((SMALL - 2, bias.shape[1]), bf16)
    sent[base : base + SMALL] = jnp.concatenate([high, low, zeros], axis=0)


def pack(place, attn, out, up, down, bias, targets):
    rows = out.shape[0] + 2 * up.shape[0] + SMALL
    return kernel_call(
        pack_body,
        [struct(attn.shape[0], HEAD, bf16), struct(rows, HEAD, bf16), struct(targets.shape[1], HEAD, bf16)],
        (place, attn, out, up, down, bias, targets),
        8,
        PACK_MICROS,
        "pack",
        in_specs=[SMEM] + [VMEM] * 6,
    )


def weight_rows(left, right):
    share = left.shape[0] // 3
    return jnp.concatenate(
        [block[m * share : (m + 1) * share] for m in range(3) for block in (left, right)], axis=0
    )


def project_into(normed, left, right, query, key, value):
    weights = weight_rows(left[...], right[...])
    size = weights.shape[0] // 3
    rows = query.shape[1]
    query[...] = contract(weights[:size], normed[:rows], 1, 1).astype(bf16)
    both = contract(weights[size:], normed, 1, 1).astype(bf16)
    key[...] = both[:size]
    row = lax.broadcasted_iota(jnp.int32, (HPAD - HDIM, normed.shape[0]), 0)
    ends = jnp.where(row < 2, 1.0, 0.0).astype(bf16)
    for h in range(size // HDIM):
        value[h * HPAD : h * HPAD + HDIM] = both[size + h * HDIM : size + (h + 1) * HDIM]
        value[h * HPAD + HDIM : (h + 1) * HPAD] = ends


def project_near_body(
    place, frames, got, frames_other, got_other, vectors, left, right, query, key, value, first, every
):
    quarter = got.shape[0]
    for j, source in enumerate((frames, got, frames_other, got_other)):
        part = source[place[0]] if j % 2 == 0 else source[...]
        rows = slice(j * quarter, (j + 1) * quarter)
        every[rows] = part
        first[rows] = (normalise(part.astype(f32))[0] * vectors[0:1] + vectors[1:2]).astype(bf16)
    project_into(first[...], left, right, query, key, value)


def projected(rows, length, size):
    return [
        struct(size, rows, bf16),
        struct(size, length, bf16),
        struct(size // HDIM * HPAD, length, bf16),
    ]


def project_near(place, frames, got, frames_other, got_other, vectors, left, right):
    quarter, model = got.shape
    size = 2 * left.shape[0] // 3
    return kernel_call(
        project_near_body,
        projected(2 * quarter, 4 * quarter, size) + [struct(4 * quarter, model, bf16)] * 2,
        (place, frames, got, frames_other, got_other, vectors, left, right),
        16,
        4,
        "project_near",
        in_specs=[SMEM] + [VMEM] * 7,
    )


def project_far_body(first, *refs):
    project_into(first[...], *refs)


def project_far(first, left, right):
    length = first.shape[0]
    size = 2 * left.shape[0] // 3
    return kernel_call(
        project_far_body,
        projected(length // 2, length, size),
        (first, left, right),
        12,
        3,
        "project_far",
    )


def by_rows(function, *values):
    pieces = [
        function(*(v[start : start + ROWS] for v in values)) for start in range(0, values[0].shape[0], ROWS)
    ]
    return [jnp.concatenate(parts, axis=0) for parts in zip(*pieces)]


def middle_body(
    place, attended_near, attended_far, frames, targets, goal_got, keep, vectors, head, *refs
):
    blocks = refs[:4]
    grad_middle_out, grad_near, grad_far, kept_out, sent_out, small_out = refs[4:10]
    second_all, ffn_all, final_all, pred_all, attn_all, hidden_all, pre_all, goal, bias_sums = refs[10:]
    rows = grad_middle_out.shape[0]
    quarter = targets.shape[1]
    deep = head.shape[0]
    share = grad_near.shape[0] // 2
    base = share + 2 * deep
    half = 2 * share
    goal[:quarter] = targets[place[1]]
    goal[quarter:] = goal_got[...]
    gain, shift = vectors[4:5], vectors[5:6]
    scale_one, scale_two = vectors[3:4], vectors[7:8]
    out_low = jnp.concatenate([b[:share] for b in blocks], axis=0)
    head_low = head[...].astype(bf16)
    small_out[...] = jnp.zeros_like(small_out)
    bias_sums[...] = jnp.zeros_like(bias_sums)

    def block_step(step, carry):
        here = aligned(step, BLOCK)

        def add(row, values):
            small_out[row : row + 1] += column_sum(values)

        mixed = contract(attended_near[:, here], out_low[:half], 0, 0) + contract(
            attended_far[:, here], out_low[half:], 0, 0
        )

        def first_norm(mixed, frames):
            biased = mixed + vectors[2:3]
            middle = frames.astype(f32) + scale_one * biased
            normed, inverse = normalise(middle)
            return biased, middle, normed, inverse, (normed * gain + shift).astype(bf16)

        biased_one, middle, normed, inverse, second = by_rows(first_norm, mixed, frames[here])
        second_all[here] = second
        slopes = []
        mixed = None
        for j, block in enumerate(blocks):
            parts = block[base : base + SMALL].astype(f32)
            bias = parts[0:1] + parts[1:2]

            def gelu(pre):
                pre = pre + bias
                square = pre * pre
                tanh = jnp.tanh(pre * (GELU_A + (GELU_A * GELU_B) * square))
                phi = 0.5 + 0.5 * tanh
                curve = (1.0 - tanh * tanh) * (0.5 * GELU_A + (1.5 * GELU_A * GELU_B) * square)
                return (pre * phi).astype(bf16), phi + pre * curve

            hidden, slope = by_rows(gelu, contract(second, block[share : share + deep], 1, 0))
            hidden_all[j, here] = hidden
            slopes.append(slope)
            part = contract(hidden, block[share + deep : base], 1, 1)
            mixed = part if j == 0 else mixed + part

        def second_scale(mixed, middle):
            biased = mixed + vectors[6:7]
            return biased, (middle + scale_two * biased).astype(bf16)

        biased_two, final = by_rows(second_scale, mixed, middle)
        final_all[here] = final

        def error(pred, goal):
            diff = pred + vectors[8:9] - goal.astype(f32)
            smooth = jnp.sqrt(diff * diff + 1.0)
            add(7, keep[...] * (smooth - 1.0) / HEAD)
            grad = (keep[...] * (diff / smooth) / HEAD).astype(bf16)
            add(6, grad.astype(f32))
            return (grad,)

        (grad_pred,) = by_rows(error, contract(final, head_low, 1, 0), goal[here])
        pred_all[here] = grad_pred

        grad_final = contract(grad_pred, head_low, 1, 1)

        def scale_back(grad, biased):
            ffn = grad * scale_two
            add(4, ffn)
            add(5, grad * biased)
            return (ffn.astype(bf16),)

        (ffn_low,) = by_rows(scale_back, grad_final, biased_two)
        ffn_all[here] = ffn_low
        grad_second = None
        for j, block in enumerate(blocks):

            def gelu_back(grad, slope):
                low = (grad * slope).astype(bf16)
                bias_sums[j : j + 1] += column_sum(low.astype(f32))
                return (low,)

            grad = contract(ffn_low, block[share + deep : base], 1, 0)
            (low,) = by_rows(gelu_back, grad, slopes[j])
            pre_all[j, here] = low
            part = contract(low, block[share : share + deep], 1, 1)
            grad_second = part if j == 0 else grad_second + part

        def norm_back(grad, normed, inverse, grad_final, biased):
            add(2, grad * normed)
            add(3, grad)
            scaled = grad * gain
            back = inverse * (scaled - row_mean(scaled) - normed * row_mean(scaled * normed))
            total = grad_final + back
            attn = total * scale_one
            add(0, attn)
            add(1, total * biased)
            return total, attn.astype(bf16)

        grad_middle, attn_low = by_rows(norm_back, grad_second, normed, inverse, grad_final, biased_one)
        grad_middle_out[here] = grad_middle
        attn_all[here] = attn_low
        grad_near[:, here] = contract(out_low[:half], attn_low, 1, 1).astype(bf16)
        grad_far[:, here] = contract(out_low[half:], attn_low, 1, 1).astype(bf16)
        return carry

    lax.fori_loop(0, rows // BLOCK, block_step, 0)

    attn_low = attn_all[...]
    grad_out = jnp.concatenate(
        [contract(attended_near[...], attn_low, 1, 0), contract(attended_far[...], attn_low, 1, 0)], axis=0
    ).astype(bf16)
    for j in range(4):
        target = (kept_out, sent_out)[j % 2]
        start = (j // 2) * base
        target[start : start + share] = grad_out[j * share : (j + 1) * share]
        target[start + share : start + share + deep] = contract(second_all[...], pre_all[j], 0, 0).astype(bf16)
        target[start + share + deep : start + base] = contract(ffn_all[...], hidden_all[j], 0, 0).astype(bf16)
        small_out[pl.ds(8 + lax.bitwise_xor(place[0], j), 1)] = bias_sums[j : j + 1]
    grad_head = contract(final_all[...], pred_all[...], 0, 0).astype(bf16)
    column = lax.broadcasted_iota(jnp.int32, (1, HEAD), 1)
    loss = jnp.sum(small_out[7:8], axis=1, keepdims=True)
    small_out[7:8] = jnp.where(column == 0, loss, 0.0)
    core = lax.rem(place[0], 2)
    size = deep // 2
    for target, first in ((kept_out, core == 0), (sent_out, core == 1)):
        target[2 * base : 2 * base + size] = jnp.where(first, grad_head[:size], grad_head[size:])
        target[2 * base + size :] = jnp.zeros((2 * SMALL, HEAD), bf16)


def middle_step(place, attended_near, attended_far, frames, targets, goal_got, keep, vectors, head, blocks):
    rows, model = frames.shape[0] // 2, frames.shape[1]
    base = blocks[0].shape[0] - SMALL
    count = 2 * base + HEAD // 2 + 2 * SMALL
    inputs = (place, attended_near, attended_far, frames, targets, goal_got, keep, vectors, head, *blocks)
    return kernel_call(
        middle_body,
        [
            struct(rows, model, f32),
            struct(*attended_near.shape, bf16),
            struct(*attended_far.shape, bf16),
            struct(count, HEAD, bf16),
            struct(count, HEAD, bf16),
            struct(SMALL, HEAD, f32),
        ],
        inputs,
        MIDDLE_LIMIT,
        20,
        "middle_step",
        in_specs=[SMEM] + [VMEM] * 12,
        scratch=[
            *[pltpu.VMEM((rows, model), bf16)] * 5,
            pltpu.VMEM((4, rows, HEAD), bf16),
            pltpu.VMEM((4, rows, HEAD), bf16),
            pltpu.VMEM((rows, HEAD), bf16),
            pltpu.VMEM((8, HEAD), f32),
        ],
    )


def fold_body(plan, place, left, right, *targets):
    for target, ranges in zip(targets, plan):
        base = 0
        for start, stop, *choice in ranges:
            if choice:
                size = (stop - start) // 2
                source = pl.ds(pl.multiple_of(start + choice[0](place) * size, SMALL), size)
            else:
                size = stop - start
                source = pl.ds(start, size)
            total = left[source].astype(f32) + right[source].astype(f32)
            target[base : base + size] = total.astype(target.dtype)
            base += size


def fold(left, right, plan, place=None, dtype=bf16):
    shapes = [
        struct(sum((r[1] - r[0]) // (2 if len(r) > 2 else 1) for r in ranges), left.shape[1], dtype)
        for ranges in plan
    ]
    if place is None:
        place = jnp.zeros((1,), jnp.int32)
    return kernel_call(
        functools.partial(fold_body, plan),
        shapes,
        (place, left, right),
        6,
        0.3,
        "fold",
        in_specs=[SMEM, VMEM, VMEM],
    )


def join_body(bit, place, kept, got, both):
    size = kept.shape[0]
    both[pl.ds(pl.multiple_of(bit(place) * size, SMALL), size)] = kept[...]
    both[pl.ds(pl.multiple_of((1 - bit(place)) * size, SMALL), size)] = got[...]


def join(kept, got, bit, place):
    return kernel_call(
        functools.partial(join_body, bit),
        struct(2 * kept.shape[0], kept.shape[1], kept.dtype),
        (place, kept, got),
        6,
        0.3,
        "join",
        in_specs=[SMEM, VMEM, VMEM],
    )


def gather_rows(parts):
    return jnp.concatenate([p[...] for p in parts], axis=0)


def weight_grads(grads, first, kept, sent, base=0):
    queries, keys, values = grads
    rows = queries[0].shape[1]
    query = contract(gather_rows(queries), first[:rows], 1, 0)
    both = contract(gather_rows(keys + values), first[...], 1, 0)
    share = query.shape[0] // 2
    for m in range(3):
        for j, target in enumerate((kept, sent)):
            start = (max(m - 1, 0) * 2 + j) * share
            part = (query if m == 0 else both)[start : start + share]
            target[m * share : (m + 1) * share] = part.astype(bf16)


def far_grads_body(calls, first, *refs):
    grads = [refs[k * calls : (k + 1) * calls] for k in range(3)]
    weight_grads(grads, first[...], *refs[3 * calls :])


def far_grads(grads, first):
    queries, keys, values = zip(*grads)
    count = 3 * sum(q.shape[0] for q in queries) // 2
    return kernel_call(
        functools.partial(far_grads_body, len(grads)),
        [struct(count, HEAD, bf16)] * 2,
        (first, *queries, *keys, *values),
        12,
        4,
        "far_grads",
    )


def post_body(calls, *refs):
    queries, keys, values = (refs[k * calls : (k + 1) * calls] for k in range(3))
    near = calls // 2
    first, frames, vectors, small_in = refs[3 * calls : 3 * calls + 4]
    blocks = refs[3 * calls + 4 : 3 * calls + 8]
    mine, other, kept, sent, small = refs[3 * calls + 8 :]
    share = blocks[0].shape[0] // 3
    rows = mine.shape[0]

    def rows_of(m):
        return jnp.concatenate([b[m * share : (m + 1) * share] for b in blocks], axis=0)

    weight_grads((queries[:near], keys[:near], values[:near]), first[...], kept, sent)
    both = jnp.concatenate([rows_of(1), rows_of(2)], axis=0)
    grads = gather_rows(keys + values)
    total = contract(grads[:, :rows], both, 0, 0) + contract(gather_rows(queries), rows_of(0), 0, 0)
    rest = contract(grads[:, rows:], both, 0, 0)
    mine[...] = total
    other[...] = rest.astype(bf16)
    normed = normalise(frames[:rows].astype(f32))[0]
    normed_rest = normalise(frames[rows:].astype(f32))[0]
    small[...] = small_in[...]
    small[12:13] = column_sum(total * normed) + column_sum(rest * normed_rest)
    small[13:14] = column_sum(total) + column_sum(rest)


def post_step(grads, first, frames, vectors, small, blocks):
    length, model = first.shape
    rows = length // 2
    queries, keys, values = zip(*grads)
    payload = struct(blocks[0].shape[0], model, bf16)
    return kernel_call(
        functools.partial(post_body, len(grads)),
        [struct(rows, model, f32), struct(rows, model, bf16), payload, payload, struct(*small.shape, f32)],
        (*queries, *keys, *values, first, frames, vectors, small, *blocks),
        POST_LIMIT,
        8,
        "post_step",
    )


def finish_body(mine, got, frames, vectors, grad_middle, own, returned):
    rows = mine.shape[0]
    grad = mine[...] + got[...].astype(f32)
    normed, inverse = normalise(frames[:rows].astype(f32))
    scaled = grad * vectors[0:1]
    back = inverse * (scaled - row_mean(scaled) - normed * row_mean(scaled * normed))
    total = grad_middle[...] + back
    quarter = own.shape[0]
    own[...] = total[:quarter]
    returned[...] = total[quarter:].astype(bf16)


def finish(mine, got, frames, vectors, grad_middle):
    rows, model = mine.shape
    return kernel_call(
        finish_body,
        [struct(rows // 2, model, f32), struct(rows // 2, model, bf16)],
        (mine, got, frames, vectors, grad_middle),
        16,
        3,
        "finish",
    )


def update(weight, moment, average, grad):
    moment_new = MOMENTUM_RATE * moment + grad
    weight_new = weight - LEARN_RATE * (grad + MOMENTUM_RATE * moment_new)
    average_new = AVERAGE_RATE * average + (1.0 - AVERAGE_RATE) * weight_new
    return (weight_new, moment_new, average_new)


CORE_PAIRS = [(0, 1), (1, 0), (2, 3), (3, 2)]
CHIP_PAIRS = [(0, 2), (2, 0), (1, 3), (3, 1)]
FORWARD_LIMIT = 28
BACKWARD_LIMIT = 28
MIDDLE_LIMIT = 36
POST_LIMIT = 20
PACK_MICROS = 3


def swap_core(values):
    return lax.ppermute(values, "tp", CORE_PAIRS)


def swap_chip(values):
    return lax.ppermute(values, "tp", CHIP_PAIRS)


def swap_dp(values, step, size):
    return lax.ppermute(values, "dp", [(i, i ^ step) for i in range(size)])


def pick(stacked, place):
    return lax.dynamic_index_in_dim(stacked, place, 0, False)


def tie(value, *others):
    return lax.optimization_barrier((value, *others))[0]


def per_device(
    frames,
    targets,
    presence,
    order,
    attn_proj,
    out_proj,
    up_proj,
    up_bias,
    down_proj,
    head_proj,
    vectors,
    momentum_attn,
    momentum_out,
    momentum_up,
    momentum_bias,
    momentum_down,
    momentum_head,
    momentum_vectors,
    average_attn,
    average_out,
    average_up,
    average_bias,
    average_down,
    average_head,
    average_vectors,
):
    size = lax.axis_size("dp")
    place = lax.axis_index("tp")
    chip, core = place // 2, place % 2
    share, deep = out_proj.shape[0], up_proj.shape[0]
    got = swap_chip(take(frames, (1 - chip).reshape(1)))
    frames_other = swap_core(frames)
    attn_own, sent, goal = pack(
        order[0, 1 - chip].reshape(1),
        jnp.swapaxes(attn_proj, 1, 2).reshape(3 * share, HEAD),
        out_proj,
        up_proj,
        down_proj,
        up_bias[None],
        targets,
    )
    attn_core = swap_core(attn_own)
    sent_core = swap_core(sent)
    got_other = swap_core(got)
    attn_chip = swap_chip(tie(attn_own, got))
    query, key, value, first, every = project_near(
        chip.reshape(1), frames, got, frames_other, got_other, vectors, attn_own, attn_core
    )
    sent_chip = swap_chip(tie(sent, first))
    near = (query, key, value)
    near_out = attention_forward(*near)
    attn_both = swap_core(tie(attn_chip, first))
    far = project_far(tie(first, near_out[0]), attn_chip, attn_both)
    sent_both = swap_core(tie(sent_chip, far[0]))
    goal_got = swap_chip(tie(goal, far[0]))
    far_out = attention_forward(*far, near_out[2])
    keep = jnp.repeat(pick(presence, chip).astype(f32), CHN)[None, :]
    where = jnp.stack([place, order[0, chip]])
    grad_middle, grad_near, grad_far, kept, sent, small = middle_step(
        where, near_out[0], far_out[0], every, targets, goal_got, keep, vectors, head_proj,
        (sent, sent_core, sent_chip, sent_both),
    )

    inputs = ((*near, near_out[0], grad_near, near_out[1], far_out[2]), (*far, far_out[0], grad_far, *far_out[1:]))
    here = near[0].shape[0] // HDIM

    def backward(part, first_head, heads, *after):
        query, *others = inputs[part]
        return attention_backward(first_head, part * here + first_head, heads, tie(query, *after), *others)

    block = share + 2 * deep
    half = HEAD // 2
    full = block + half + 2 * SMALL
    spot = lax.axis_index("dp").reshape(1)
    bits = [lambda p: p[0] % 2, lambda p: p[0] // 2 % 2]
    others = [lambda p: 1 - p[0] % 2, lambda p: 1 - p[0] // 2 % 2]
    steps = [1 << k for k in range(size.bit_length() - 1)]
    last_rows = (2 * block, full + block)
    rows = 3 * share

    got_core = swap_core(sent)
    kept, sent = fold(
        kept, got_core, [[(0, block), last_rows], [(block, 2 * block), last_rows]]
    )
    got_chip = swap_chip(sent)
    far_one = backward(1, 0, here // 2, sent)
    far_two = backward(1, here // 2, here // 2, far_one[0])
    kept, sent = fold(
        kept, tie(got_chip, far_two[0]), [[(0, full, bits[0])], [(0, full, others[0])]], spot
    )
    got_y = swap_dp(sent, 1, size)
    far_kept, far_sent = far_grads([far_one, far_two], tie(first, sent))
    got_far = swap_core(far_sent)
    near_one = backward(0, 0, here // 2, sent, far_sent)
    (far_kept,) = fold(far_kept, tie(got_far, near_one[0]), [[(0, rows)]])
    got_far = swap_chip(far_kept)
    (kept,) = fold(kept, tie(got_y, near_one[0]), [[(0, full // 2)]])
    got_z = swap_dp(kept, 2, size)
    near_two = backward(0, here // 2, here // 2, kept, far_kept)
    (kept,) = fold(kept, tie(got_z, near_two[0]), [[(0, full // 2)]])
    got_step = swap_dp(kept, steps[2], size)
    mine, other, near_kept, near_sent, small = post_step(
        [near_one, near_two, far_one, far_two],
        tie(first, kept, got_far),
        every,
        vectors,
        small,
        (attn_own, attn_core, attn_chip, attn_both),
    )
    got_near = swap_core(near_sent)
    got_small = swap_core(small)
    other_rows = swap_core(other)
    (near_kept,) = fold(near_kept, got_far, [[(0, rows)]], dtype=f32)
    (attn_kept,) = fold(near_kept, got_near, [[(0, rows)]])
    got_attn = swap_dp(attn_kept, 1, size)
    (small,) = fold(small, tie(got_small, attn_kept), [[(0, SMALL)]], dtype=f32)
    got_small = swap_chip(small)
    own_rows, returned = finish(mine, other_rows, every, vectors, tie(grad_middle, attn_kept, small))
    returned = swap_chip(returned)
    (small,) = fold(small, tie(got_small, own_rows), [[(0, SMALL)]], dtype=f32)
    for step in steps:
        got_small = swap_dp(small, step, size)
        (attn_kept,) = fold(
            attn_kept, tie(got_attn, small), [[(0, rows)]], dtype=f32 if step == steps[-1] else bf16
        )
        if step < steps[-1]:
            got_attn = swap_dp(attn_kept, 2 * step, size)
        if step == 2:
            for high in steps[2:]:
                got_step = tie(got_step, attn_kept) if high == steps[2] else swap_dp(kept, high, size)
                (kept,) = fold(kept, got_step, [[(0, full // 2)]])
            got_kept = swap_dp(kept, 1, size)
            returned = tie(returned, attn_kept)
        (small,) = fold(small, tie(got_small, attn_kept), [[(0, SMALL)]], dtype=f32)
    kept = join(kept, got_kept, bits[0], spot)

    returned = returned.astype(f32)
    grad_frames = jnp.where(
        chip == 0, jnp.stack([own_rows, returned]), jnp.stack([returned, own_rows])
    )
    kept = kept.astype(f32)
    grad_out = kept[:share]
    grad_up = kept[share : share + deep]
    grad_down = kept[share + deep : block]
    head_mine = kept[block : block + half]
    head_other = swap_core(head_mine.astype(bf16)).astype(f32)
    grad_head = jnp.where(
        core == 0,
        jnp.concatenate([head_mine, head_other], axis=0),
        jnp.concatenate([head_other, head_mine], axis=0),
    )
    grad_attn_proj = jnp.swapaxes(attn_kept.reshape(3, share, HEAD), 1, 2)
    loss = small[7, 0]
    grad_up_bias = pick(small[8:12], place)
    grad_vectors = jnp.concatenate([small[12:14], small[:7]], axis=0)
    first_set = update(attn_proj, momentum_attn, average_attn, grad_attn_proj)
    second_set = update(out_proj, momentum_out, average_out, grad_out)
    third_set = update(up_proj, momentum_up, average_up, grad_up)
    fourth_set = update(up_bias, momentum_bias, average_bias, grad_up_bias)
    fifth_set = update(down_proj, momentum_down, average_down, grad_down)
    sixth_set = update(head_proj, momentum_head, average_head, grad_head)
    seventh_set = update(vectors, momentum_vectors, average_vectors, grad_vectors)
    return (
        loss,
        first_set[0],
        second_set[0],
        third_set[0],
        fourth_set[0],
        fifth_set[0],
        sixth_set[0],
        seventh_set[0],
        first_set[1],
        second_set[1],
        third_set[1],
        fourth_set[1],
        fifth_set[1],
        sixth_set[1],
        seventh_set[1],
        first_set[2],
        second_set[2],
        third_set[2],
        fourth_set[2],
        fifth_set[2],
        sixth_set[2],
        seventh_set[2],
        grad_frames,
    )


def solution(mesh):
    in_specs = (
        P("dp", "tp", None),
        P("dp", "tp", None),
        P("dp", None),
        P("dp", None),
        P(None, None, "tp"),
        P("tp", None),
        P(None, "tp"),
        P("tp"),
        P(None, "tp"),
        P(),
        P(),
        P(None, None, "tp"),
        P("tp", None),
        P(None, "tp"),
        P("tp"),
        P(None, "tp"),
        P(),
        P(),
        P(None, None, "tp"),
        P("tp", None),
        P(None, "tp"),
        P("tp"),
        P(None, "tp"),
        P(),
        P(),
    )
    out_specs = (
        P(),
        P(None, None, "tp"),
        P("tp", None),
        P(None, "tp"),
        P("tp"),
        P(None, "tp"),
        P(),
        P(),
        P(None, None, "tp"),
        P("tp", None),
        P(None, "tp"),
        P("tp"),
        P(None, "tp"),
        P(),
        P(),
        P(None, None, "tp"),
        P("tp", None),
        P(None, "tp"),
        P("tp"),
        P(None, "tp"),
        P(),
        P(),
        P("dp", "tp", None),
    )
    return jax.shard_map(
        per_device, mesh=mesh, in_specs=in_specs, out_specs=out_specs, check_vma=False
    )
```

```python
import functools
import math

import jax
import jax.numpy as jnp
from jax import lax
from jax.experimental import pallas as pl
from jax.experimental.pallas import tpu as pltpu
from jax.sharding import PartitionSpec as P

CHN = 96
HDIM = 48
HPAD = 64
HEAD = 384


EPSILON = 1e-05
MOMENTUM_RATE = 0.9
LEARN_RATE = 0.02
AVERAGE_RATE = 0.9
SCALE = HDIM ** (-0.5)
LOG_SCALE = SCALE * math.log2(math.e)
GELU_A = math.sqrt(2.0 / math.pi)
GELU_B = 0.044715
SMALL = 16
BLOCK = 384
ROWS = 64
CHUNKS = 3

bf16 = jnp.bfloat16
f32 = jnp.float32
HBM = pl.BlockSpec(memory_space=pltpu.HBM)
SMEM = pl.BlockSpec(memory_space=pltpu.SMEM)
VMEM = pl.BlockSpec(memory_space=pltpu.VMEM)


def kernel_call(body, outs, inputs, limit, micros, name, in_specs=None, out_specs=None, scratch=(), aliases=None):
    return pl.pallas_call(
        body,
        out_shape=outs,
        in_specs=in_specs or [VMEM] * len(inputs),
        out_specs=out_specs or jax.tree.map(lambda _: VMEM, outs),
        scratch_shapes=list(scratch),
        input_output_aliases=aliases or {},
        compiler_params=pltpu.CompilerParams(vmem_limit_bytes=limit << 20),
        cost_estimate=pl.CostEstimate(flops=int(micros * 1e9), bytes_accessed=0, transcendentals=0),
        name=name,
    )(*inputs)


def struct(rows, columns, dtype):
    return jax.ShapeDtypeStruct((rows, columns), dtype)


def contract(left, right, left_dim, right_dim):
    return lax.dot_general(
        left, right, (((left_dim,), (right_dim,)), ((), ())), preferred_element_type=f32
    )


def row_mean(values):
    return jnp.mean(values, axis=-1, keepdims=True)


def column_sum(values):
    return jnp.sum(values, axis=0, keepdims=True)


def normalise(values):
    centred = values - row_mean(values)
    inverse = lax.rsqrt(row_mean(centred * centred) + EPSILON)
    return centred * inverse, inverse


def aligned(index, size):
    return pl.ds(pl.multiple_of(index * size, size), size)


def forward_body(first, heads, query, key, value, *refs):
    mixed, totals, weights, slots, sems = refs[-5:]

    def out_copy(h):
        slot = lax.rem(h, 2)
        return pltpu.make_async_copy(slots.at[slot], weights.at[h + first], sems.at[slot])

    def head(h, carry):
        @pl.when(h >= 2)
        def _():
            out_copy(h - 2).wait()

        rows = aligned(h, HDIM)
        scores = contract(query[rows], key[rows], 0, 0)
        maximum = jnp.max(scores, axis=1, keepdims=True)
        exponent = jnp.exp2((scores - maximum) * LOG_SCALE).astype(bf16)
        slots[lax.rem(h, 2)] = exponent
        out_copy(h).start()
        summed = contract(value[aligned(h, HPAD)], exponent, 1, 1)
        total = summed[HDIM : HDIM + 1]
        mixed[rows] = (summed[:HDIM] / total).astype(bf16)
        totals[pl.ds(h, 1)] = total
        return carry

    lax.fori_loop(0, heads, head, 0)
    for h in range(max(0, heads - 2), heads):
        out_copy(h).wait()


def attention_forward(query, key, value, weights=None):
    heads = query.shape[0] // HDIM
    first = 0 if weights is None else heads
    rows, length = query.shape[1], key.shape[1]
    return kernel_call(
        functools.partial(forward_body, first, heads),
        [
            struct(heads * HDIM, rows, bf16),
            struct(heads, rows, f32),
            jax.ShapeDtypeStruct((2 * heads, rows, length), bf16),
        ],
        (query, key, value) if weights is None else (query, key, value, weights),
        FORWARD_LIMIT,
        4 * heads,
        "attention_forward",
        in_specs=[VMEM] * 3 if weights is None else [VMEM] * 3 + [HBM],
        aliases={} if weights is None else {3: 2},
        out_specs=[VMEM, VMEM, HBM],
        scratch=[pltpu.VMEM((2, rows, length), bf16), pltpu.SemaphoreType.DMA((2,))],
    )


def backward_body(
    first, base, heads, query, key, value, mixed, grad_mixed, totals, weights,
    grad_query, grad_key, grad_value, slots, sums, scaled_all, sems
):
    def in_copy(h):
        slot = lax.rem(h, 2)
        return pltpu.make_async_copy(weights.at[h + base], slots.at[slot], sems.at[slot])

    in_copy(0).start()
    width = key.shape[1] // CHUNKS

    def head(h, carry):
        @pl.when(h + 1 < heads)
        def _():
            in_copy(h + 1).start()

        rows, here = aligned(h + first, HDIM), aligned(h, HDIM)
        inverse = 1.0 / totals[pl.ds(h + first, 1)]
        grad = grad_mixed[rows].astype(f32)
        delta = column_sum(grad * mixed[rows].astype(f32))
        scaled = (grad * inverse).astype(bf16)
        offset = -delta * inverse
        high = offset.astype(bf16).astype(f32)
        row = lax.broadcasted_iota(jnp.int32, (HPAD - HDIM, offset.shape[1]), 0)
        extra = jnp.where(row == 0, high, jnp.where(row == 1, offset - high, 0.0)).astype(bf16)
        scaled_all[...] = jnp.concatenate([scaled, extra], axis=0)
        sums[...] = jnp.zeros_like(sums)
        in_copy(h).wait()

        def chunk(i, carry):
            part = aligned(i, width)
            grad_weights = contract(scaled_all[...], value[aligned(h + first, HPAD), part], 0, 0)
            kept = slots[lax.rem(h, 2), :, part]
            grad_scores = (kept.astype(f32) * grad_weights).astype(bf16)
            sums[...] += contract(key[rows, part], grad_scores, 1, 1)
            grad_key[here, part] = (contract(query[rows], grad_scores, 1, 0) * SCALE).astype(bf16)
            grad_value[here, part] = contract(scaled_all[:HDIM], kept, 1, 0).astype(bf16)
            return carry

        lax.fori_loop(0, CHUNKS, chunk, 0)
        grad_query[here] = (sums[...] * SCALE).astype(bf16)
        return carry

    lax.fori_loop(0, heads, head, 0)


def attention_backward(first, base, heads, query, key, value, mixed, grad_mixed, totals, weights):
    rows, length = query.shape[1], key.shape[1]
    return kernel_call(
        functools.partial(backward_body, first, base, heads),
        [
            struct(heads * HDIM, rows, bf16),
            struct(heads * HDIM, length, bf16),
            struct(heads * HDIM, length, bf16),
        ],
        (query, key, value, mixed, grad_mixed, totals, weights),
        BACKWARD_LIMIT,
        5.5 * heads,
        "attention_backward",
        in_specs=[VMEM] * 6 + [HBM],
        scratch=[
            pltpu.VMEM((2, rows, length), bf16),
            pltpu.VMEM((HDIM, rows), f32),
            pltpu.VMEM((HPAD, rows), bf16),
            pltpu.SemaphoreType.DMA((2,)),
        ],
    )


def take_body(place, stacked, taken):
    taken[...] = stacked[place[0]]


def take(stacked, place):
    count, rows, columns = stacked.shape
    return kernel_call(
        take_body, struct(rows, columns, stacked.dtype), (place, stacked), 2, 1, "take", in_specs=[SMEM, VMEM]
    )


def pack_body(place, attn, out, up, down, bias, targets, attn_low, sent, goal):
    share, deep = out.shape[0], up.shape[0]
    base = share + 2 * deep
    goal[...] = targets[place[0]]
    attn_low[...] = attn[...].astype(bf16)
    sent[:share] = out[...].astype(bf16)
    sent[share : share + deep] = up[...].astype(bf16)
    sent[share + deep : base] = down[...].astype(bf16)
    high = bias[...].astype(bf16)
    low = (bias[...] - high.astype(f32)).astype(bf16)
    zeros = jnp.zeros((SMALL - 2, bias.shape[1]), bf16)
    sent[base : base + SMALL] = jnp.concatenate([high, low, zeros], axis=0)


def pack(place, attn, out, up, down, bias, targets):
    rows = out.shape[0] + 2 * up.shape[0] + SMALL
    return kernel_call(
        pack_body,
        [struct(attn.shape[0], HEAD, bf16), struct(rows, HEAD, bf16), struct(targets.shape[1], HEAD, bf16)],
        (place, attn, out, up, down, bias, targets),
        8,
        PACK_MICROS,
        "pack",
        in_specs=[SMEM] + [VMEM] * 6,
    )


def weight_rows(left, right):
    share = left.shape[0] // 3
    return jnp.concatenate(
        [block[m * share : (m + 1) * share] for m in range(3) for block in (left, right)], axis=0
    )


def project_into(normed, left, right, query, key, value):
    weights = weight_rows(left[...], right[...])
    size = weights.shape[0] // 3
    rows = query.shape[1]
    query[...] = contract(weights[:size], normed[:rows], 1, 1).astype(bf16)
    both = contract(weights[size:], normed, 1, 1).astype(bf16)
    key[...] = both[:size]
    row = lax.broadcasted_iota(jnp.int32, (HPAD - HDIM, normed.shape[0]), 0)
    ends = jnp.where(row < 2, 1.0, 0.0).astype(bf16)
    for h in range(size // HDIM):
        value[h * HPAD : h * HPAD + HDIM] = both[size + h * HDIM : size + (h + 1) * HDIM]
        value[h * HPAD + HDIM : (h + 1) * HPAD] = ends


def project_near_body(
    place, frames, got, frames_other, got_other, vectors, left, right, query, key, value, first, every
):
    quarter = got.shape[0]
    for j, source in enumerate((frames, got, frames_other, got_other)):
        part = source[place[0]] if j % 2 == 0 else source[...]
        rows = slice(j * quarter, (j + 1) * quarter)
        every[rows] = part
        first[rows] = (normalise(part.astype(f32))[0] * vectors[0:1] + vectors[1:2]).astype(bf16)
    project_into(first[...], left, right, query, key, value)


def projected(rows, length, size):
    return [
        struct(size, rows, bf16),
        struct(size, length, bf16),
        struct(size // HDIM * HPAD, length, bf16),
    ]


def project_near(place, frames, got, frames_other, got_other, vectors, left, right):
    quarter, model = got.shape
    size = 2 * left.shape[0] // 3
    return kernel_call(
        project_near_body,
        projected(2 * quarter, 4 * quarter, size) + [struct(4 * quarter, model, bf16)] * 2,
        (place, frames, got, frames_other, got_other, vectors, left, right),
        16,
        4,
        "project_near",
        in_specs=[SMEM] + [VMEM] * 7,
    )


def project_far_body(first, *refs):
    project_into(first[...], *refs)


def project_far(first, left, right):
    length = first.shape[0]
    size = 2 * left.shape[0] // 3
    return kernel_call(
        project_far_body,
        projected(length // 2, length, size),
        (first, left, right),
        12,
        3,
        "project_far",
    )


def by_rows(function, *values):
    pieces = [
        function(*(v[start : start + ROWS] for v in values)) for start in range(0, values[0].shape[0], ROWS)
    ]
    return [jnp.concatenate(parts, axis=0) for parts in zip(*pieces)]


def middle_body(
    place, attended_near, attended_far, frames, targets, goal_got, keep, vectors, head, *refs
):
    blocks = refs[:4]
    grad_middle_out, grad_near, grad_far, kept_out, sent_out, small_out = refs[4:10]
    second_all, ffn_all, final_all, pred_all, attn_all, hidden_all, pre_all, goal, bias_sums = refs[10:]
    rows = grad_middle_out.shape[0]
    quarter = targets.shape[1]
    deep = head.shape[0]
    share = grad_near.shape[0] // 2
    base = share + 2 * deep
    half = 2 * share
    goal[:quarter] = targets[place[1]]
    goal[quarter:] = goal_got[...]
    gain, shift = vectors[4:5], vectors[5:6]
    scale_one, scale_two = vectors[3:4], vectors[7:8]
    out_low = jnp.concatenate([b[:share] for b in blocks], axis=0)
    head_low = head[...].astype(bf16)
    small_out[...] = jnp.zeros_like(small_out)
    bias_sums[...] = jnp.zeros_like(bias_sums)

    def block_step(step, carry):
        here = aligned(step, BLOCK)

        def add(row, values):
            small_out[row : row + 1] += column_sum(values)

        mixed = contract(attended_near[:, here], out_low[:half], 0, 0) + contract(
            attended_far[:, here], out_low[half:], 0, 0
        )

        def first_norm(mixed, frames):
            biased = mixed + vectors[2:3]
            middle = frames.astype(f32) + scale_one * biased
            normed, inverse = normalise(middle)
            return biased, middle, normed, inverse, (normed * gain + shift).astype(bf16)

        biased_one, middle, normed, inverse, second = by_rows(first_norm, mixed, frames[here])
        second_all[here] = second
        slopes = []
        mixed = None
        for j, block in enumerate(blocks):
            parts = block[base : base + SMALL].astype(f32)
            bias = parts[0:1] + parts[1:2]

            def gelu(pre):
                pre = pre + bias
                square = pre * pre
                tanh = jnp.tanh(pre * (GELU_A + (GELU_A * GELU_B) * square))
                phi = 0.5 + 0.5 * tanh
                curve = (1.0 - tanh * tanh) * (0.5 * GELU_A + (1.5 * GELU_A * GELU_B) * square)
                return (pre * phi).astype(bf16), phi + pre * curve

            hidden, slope = by_rows(gelu, contract(second, block[share : share + deep], 1, 0))
            hidden_all[j, here] = hidden
            slopes.append(slope)
            part = contract(hidden, block[share + deep : base], 1, 1)
            mixed = part if j == 0 else mixed + part

        def second_scale(mixed, middle):
            biased = mixed + vectors[6:7]
            return biased, (middle + scale_two * biased).astype(bf16)

        biased_two, final = by_rows(second_scale, mixed, middle)
        final_all[here] = final

        def error(pred, goal):
            diff = pred + vectors[8:9] - goal.astype(f32)
            smooth = jnp.sqrt(diff * diff + 1.0)
            add(7, keep[...] * (smooth - 1.0) / HEAD)
            grad = (keep[...] * (diff / smooth) / HEAD).astype(bf16)
            add(6, grad.astype(f32))
            return (grad,)

        (grad_pred,) = by_rows(error, contract(final, head_low, 1, 0), goal[here])
        pred_all[here] = grad_pred

        grad_final = contract(grad_pred, head_low, 1, 1)

        def scale_back(grad, biased):
            ffn = grad * scale_two
            add(4, ffn)
            add(5, grad * biased)
            return (ffn.astype(bf16),)

        (ffn_low,) = by_rows(scale_back, grad_final, biased_two)
        ffn_all[here] = ffn_low
        grad_second = None
        for j, block in enumerate(blocks):

            def gelu_back(grad, slope):
                low = (grad * slope).astype(bf16)
                bias_sums[j : j + 1] += column_sum(low.astype(f32))
                return (low,)

            grad = contract(ffn_low, block[share + deep : base], 1, 0)
            (low,) = by_rows(gelu_back, grad, slopes[j])
            pre_all[j, here] = low
            part = contract(low, block[share : share + deep], 1, 1)
            grad_second = part if j == 0 else grad_second + part

        def norm_back(grad, normed, inverse, grad_final, biased):
            add(2, grad * normed)
            add(3, grad)
            scaled = grad * gain
            back = inverse * (scaled - row_mean(scaled) - normed * row_mean(scaled * normed))
            total = grad_final + back
            attn = total * scale_one
            add(0, attn)
            add(1, total * biased)
            return total, attn.astype(bf16)

        grad_middle, attn_low = by_rows(norm_back, grad_second, normed, inverse, grad_final, biased_one)
        grad_middle_out[here] = grad_middle
        attn_all[here] = attn_low
        grad_near[:, here] = contract(out_low[:half], attn_low, 1, 1).astype(bf16)
        grad_far[:, here] = contract(out_low[half:], attn_low, 1, 1).astype(bf16)
        return carry

    lax.fori_loop(0, rows // BLOCK, block_step, 0)

    attn_low = attn_all[...]
    grad_out = jnp.concatenate(
        [contract(attended_near[...], attn_low, 1, 0), contract(attended_far[...], attn_low, 1, 0)], axis=0
    ).astype(bf16)
    for j in range(4):
        target = (kept_out, sent_out)[j % 2]
        start = (j // 2) * base
        target[start : start + share] = grad_out[j * share : (j + 1) * share]
        small_out[pl.ds(8 + lax.bitwise_xor(place[0], j), 1)] = bias_sums[j : j + 1]

    def weight_step(i, carry):
        for k, target in enumerate((kept_out, sent_out)):
            start = pl.multiple_of(i * base + share, SMALL)
            up = contract(second_all[...], pre_all[2 * i + k], 0, 0).astype(bf16)
            down = contract(ffn_all[...], hidden_all[2 * i + k], 0, 0).astype(bf16)
            target[pl.ds(start, deep)] = up
            target[pl.ds(pl.multiple_of(start + deep, SMALL), deep)] = down
        return carry

    lax.fori_loop(0, 2, weight_step, 0)
    grad_head = contract(final_all[...], pred_all[...], 0, 0).astype(bf16)
    column = lax.broadcasted_iota(jnp.int32, (1, HEAD), 1)
    loss = jnp.sum(small_out[7:8], axis=1, keepdims=True)
    small_out[7:8] = jnp.where(column == 0, loss, 0.0)
    core = lax.rem(place[0], 2)
    size = deep // 2
    for target, first in ((kept_out, core == 0), (sent_out, core == 1)):
        target[2 * base : 2 * base + size] = jnp.where(first, grad_head[:size], grad_head[size:])
        target[2 * base + size :] = jnp.zeros((2 * SMALL, HEAD), bf16)


def middle_step(place, attended_near, attended_far, frames, targets, goal_got, keep, vectors, head, blocks):
    rows, model = frames.shape[0] // 2, frames.shape[1]
    base = blocks[0].shape[0] - SMALL
    count = 2 * base + HEAD // 2 + 2 * SMALL
    inputs = (place, attended_near, attended_far, frames, targets, goal_got, keep, vectors, head, *blocks)
    return kernel_call(
        middle_body,
        [
            struct(rows, model, f32),
            struct(*attended_near.shape, bf16),
            struct(*attended_far.shape, bf16),
            struct(count, HEAD, bf16),
            struct(count, HEAD, bf16),
            struct(SMALL, HEAD, f32),
        ],
        inputs,
        MIDDLE_LIMIT,
        20,
        "middle_step",
        in_specs=[SMEM] + [VMEM] * 12,
        scratch=[
            *[pltpu.VMEM((rows, model), bf16)] * 5,
            pltpu.VMEM((4, rows, HEAD), bf16),
            pltpu.VMEM((4, rows, HEAD), bf16),
            pltpu.VMEM((rows, HEAD), bf16),
            pltpu.VMEM((8, HEAD), f32),
        ],
    )


def fold_body(plan, place, left, right, *targets):
    for target, ranges in zip(targets, plan):
        base = 0
        for start, stop, *choice in ranges:
            if choice:
                size = (stop - start) // 2
                source = pl.ds(pl.multiple_of(start + choice[0](place) * size, SMALL), size)
            else:
                size = stop - start
                source = pl.ds(start, size)
            total = left[source].astype(f32) + right[source].astype(f32)
            target[base : base + size] = total.astype(target.dtype)
            base += size


def fold(left, right, plan, place=None, dtype=bf16):
    shapes = [
        struct(sum((r[1] - r[0]) // (2 if len(r) > 2 else 1) for r in ranges), left.shape[1], dtype)
        for ranges in plan
    ]
    if place is None:
        place = jnp.zeros((1,), jnp.int32)
    return kernel_call(
        functools.partial(fold_body, plan),
        shapes,
        (place, left, right),
        6,
        0.3,
        "fold",
        in_specs=[SMEM, VMEM, VMEM],
    )


def join_body(bit, place, kept, got, both):
    size = kept.shape[0]
    both[pl.ds(pl.multiple_of(bit(place) * size, SMALL), size)] = kept[...]
    both[pl.ds(pl.multiple_of((1 - bit(place)) * size, SMALL), size)] = got[...]


def join(kept, got, bit, place):
    return kernel_call(
        functools.partial(join_body, bit),
        struct(2 * kept.shape[0], kept.shape[1], kept.dtype),
        (place, kept, got),
        6,
        0.3,
        "join",
        in_specs=[SMEM, VMEM, VMEM],
    )


def gather_rows(parts):
    return jnp.concatenate([p[...] for p in parts], axis=0)


def weight_grads(grads, first, kept, sent, base=0):
    queries, keys, values = grads
    rows = queries[0].shape[1]
    query = contract(gather_rows(queries), first[:rows], 1, 0)
    both = contract(gather_rows(keys + values), first[...], 1, 0)
    share = query.shape[0] // 2
    for m in range(3):
        for j, target in enumerate((kept, sent)):
            start = (max(m - 1, 0) * 2 + j) * share
            part = (query if m == 0 else both)[start : start + share]
            target[m * share : (m + 1) * share] = part.astype(bf16)


def far_grads_body(calls, first, *refs):
    grads = [refs[k * calls : (k + 1) * calls] for k in range(3)]
    weight_grads(grads, first[...], *refs[3 * calls :])


def far_grads(grads, first):
    queries, keys, values = zip(*grads)
    count = 3 * sum(q.shape[0] for q in queries) // 2
    return kernel_call(
        functools.partial(far_grads_body, len(grads)),
        [struct(count, HEAD, bf16)] * 2,
        (first, *queries, *keys, *values),
        12,
        4,
        "far_grads",
    )


def post_body(calls, near, *refs):
    queries, keys, values = (refs[k * calls : (k + 1) * calls] for k in range(3))
    first, frames, vectors, small_in = refs[3 * calls : 3 * calls + 4]
    blocks = refs[3 * calls + 4 : 3 * calls + 8]
    mine, other, kept, sent, small = refs[3 * calls + 8 :]
    share = blocks[0].shape[0] // 3
    rows = mine.shape[0]

    def rows_of(m):
        return jnp.concatenate([b[m * share : (m + 1) * share] for b in blocks], axis=0)

    weight_grads((queries[:near], keys[:near], values[:near]), first[...], kept, sent)
    both = jnp.concatenate([rows_of(1), rows_of(2)], axis=0)
    query_rows = rows_of(0)
    small[...] = small_in[...]

    def part(step, carry):
        here = aligned(step, BLOCK)
        there = pl.ds(pl.multiple_of(rows + step * BLOCK, BLOCK), BLOCK)

        def pulled(parts, columns, weights):
            return contract(jnp.concatenate([p[:, columns] for p in parts], axis=0), weights, 0, 0)

        def ends(total, place):
            normed = normalise(frames[place].astype(f32))[0]
            small[12:13] += column_sum(total * normed)
            small[13:14] += column_sum(total)

        total = pulled(keys + values, here, both) + pulled(queries, here, query_rows)
        mine[here] = total
        ends(total, here)
        rest = pulled(keys + values, there, both)
        other[here] = rest.astype(bf16)
        ends(rest, there)
        return carry

    lax.fori_loop(0, rows // BLOCK, part, 0)


def post_step(grads, first, frames, vectors, small, blocks):
    length, model = first.shape
    rows = length // 2
    queries, keys, values = zip(*grads)
    payload = struct(blocks[0].shape[0], model, bf16)
    return kernel_call(
        functools.partial(post_body, len(grads), 2),
        [struct(rows, model, f32), struct(rows, model, bf16), payload, payload, struct(*small.shape, f32)],
        (*queries, *keys, *values, first, frames, vectors, small, *blocks),
        POST_LIMIT,
        8,
        "post_step",
    )


def finish_body(mine, got, frames, vectors, grad_middle, own, returned):
    quarter = own.shape[0]
    size = quarter // 3

    def part(step, carry):
        for target, base in ((own, 0), (returned, quarter)):
            there = aligned(step, size)
            here = pl.ds(pl.multiple_of(base + step * size, size), size)
            grad = mine[here] + got[here].astype(f32)
            normed, inverse = normalise(frames[here].astype(f32))
            scaled = grad * vectors[0:1]
            back = inverse * (scaled - row_mean(scaled) - normed * row_mean(scaled * normed))
            target[there] = (grad_middle[here] + back).astype(target.dtype)
        return carry

    lax.fori_loop(0, 3, part, 0)


def finish(mine, got, frames, vectors, grad_middle):
    rows, model = mine.shape
    return kernel_call(
        finish_body,
        [struct(rows // 2, model, f32), struct(rows // 2, model, bf16)],
        (mine, got, frames, vectors, grad_middle),
        16,
        3,
        "finish",
    )


def update(weight, moment, average, grad):
    moment_new = MOMENTUM_RATE * moment + grad
    weight_new = weight - LEARN_RATE * (grad + MOMENTUM_RATE * moment_new)
    average_new = AVERAGE_RATE * average + (1.0 - AVERAGE_RATE) * weight_new
    return (weight_new, moment_new, average_new)


CORE_PAIRS = [(0, 1), (1, 0), (2, 3), (3, 2)]
CHIP_PAIRS = [(0, 2), (2, 0), (1, 3), (3, 1)]
FORWARD_LIMIT = 28
BACKWARD_LIMIT = 28
MIDDLE_LIMIT = 30
POST_LIMIT = 20
PACK_MICROS = 3


def swap_core(values):
    return lax.ppermute(values, "tp", CORE_PAIRS)


def swap_chip(values):
    return lax.ppermute(values, "tp", CHIP_PAIRS)


def swap_dp(values, step, size):
    return lax.ppermute(values, "dp", [(i, i ^ step) for i in range(size)])


def pick(stacked, place):
    return lax.dynamic_index_in_dim(stacked, place, 0, False)


def tie(value, *others):
    return lax.optimization_barrier((value, *others))[0]


def per_device(
    frames,
    targets,
    presence,
    order,
    attn_proj,
    out_proj,
    up_proj,
    up_bias,
    down_proj,
    head_proj,
    vectors,
    momentum_attn,
    momentum_out,
    momentum_up,
    momentum_bias,
    momentum_down,
    momentum_head,
    momentum_vectors,
    average_attn,
    average_out,
    average_up,
    average_bias,
    average_down,
    average_head,
    average_vectors,
):
    size = lax.axis_size("dp")
    place = lax.axis_index("tp")
    chip, core = place // 2, place % 2
    share, deep = out_proj.shape[0], up_proj.shape[0]
    got = swap_chip(take(frames, (1 - chip).reshape(1)))
    frames_other = swap_core(frames)
    attn_own, sent, goal = pack(
        order[0, 1 - chip].reshape(1),
        jnp.swapaxes(attn_proj, 1, 2).reshape(3 * share, HEAD),
        out_proj,
        up_proj,
        down_proj,
        up_bias[None],
        targets,
    )
    attn_core = swap_core(attn_own)
    sent_core = swap_core(sent)
    got_other = swap_core(tie(got, attn_own))
    attn_chip = swap_chip(tie(attn_own, got))
    query, key, value, first, every = project_near(
        chip.reshape(1), frames, got, frames_other, got_other, vectors, attn_own, attn_core
    )
    sent_chip = swap_chip(tie(sent, first))
    near = (query, key, value)
    near_out = attention_forward(*near)
    attn_both = swap_core(tie(attn_chip, first))
    far = project_far(tie(first, near_out[0]), attn_chip, attn_both)
    sent_both = swap_core(tie(sent_chip, far[0]))
    goal_got = swap_chip(tie(goal, far[0]))
    far_out = attention_forward(*far, near_out[2])
    keep = jnp.repeat(pick(presence, chip).astype(f32), CHN)[None, :]
    where = jnp.stack([place, order[0, chip]])
    grad_middle, grad_near, grad_far, kept, sent, small = middle_step(
        where, near_out[0], far_out[0], every, targets, goal_got, keep, vectors, head_proj,
        (sent, sent_core, sent_chip, sent_both),
    )

    inputs = ((*near, near_out[0], grad_near, near_out[1], far_out[2]), (*far, far_out[0], grad_far, *far_out[1:]))
    here = near[0].shape[0] // HDIM

    def backward(part, first_head, heads, *after):
        query, *others = inputs[part]
        return attention_backward(first_head, part * here + first_head, heads, tie(query, *after), *others)

    block = share + 2 * deep
    half = HEAD // 2
    full = block + half + 2 * SMALL
    spot = lax.axis_index("dp").reshape(1)
    bits = [lambda p: p[0] % 2, lambda p: p[0] // 2 % 2]
    others = [lambda p: 1 - p[0] % 2, lambda p: 1 - p[0] // 2 % 2]
    steps = [1 << k for k in range(size.bit_length() - 1)]
    last_rows = (2 * block, full + block)
    rows = 3 * share

    got_core = swap_core(sent)
    kept, sent = fold(
        kept, got_core, [[(0, block), last_rows], [(block, 2 * block), last_rows]]
    )
    got_chip = swap_chip(sent)
    far_all = backward(1, 0, here, sent)
    kept, sent = fold(
        kept, tie(got_chip, far_all[0]), [[(0, full, bits[0])], [(0, full, others[0])]], spot
    )
    got_y = swap_dp(sent, 1, size)
    far_kept, far_sent = far_grads([far_all], tie(first, sent))
    got_far = swap_core(far_sent)
    near_one = backward(0, 0, here // 2, sent, far_sent)
    (far_kept,) = fold(far_kept, tie(got_far, near_one[0]), [[(0, rows)]])
    got_far = swap_chip(far_kept)
    (kept,) = fold(kept, tie(got_y, near_one[0]), [[(0, full // 2)]])
    got_z = swap_dp(kept, 2, size)
    near_two = backward(0, here // 2, here // 2, kept, far_kept)
    (kept,) = fold(kept, tie(got_z, near_two[0]), [[(0, full // 2)]])
    got_step = swap_dp(kept, steps[2], size)
    mine, other, near_kept, near_sent, small = post_step(
        [near_one, near_two, far_all],
        tie(first, kept, got_far),
        every,
        vectors,
        small,
        (attn_own, attn_core, attn_chip, attn_both),
    )
    got_near = swap_core(near_sent)
    got_small = swap_core(small)
    other_rows = swap_core(other)
    (near_kept,) = fold(near_kept, got_far, [[(0, rows)]], dtype=f32)
    (attn_kept,) = fold(near_kept, got_near, [[(0, rows)]])
    got_attn = swap_dp(attn_kept, 1, size)
    (small,) = fold(small, tie(got_small, attn_kept), [[(0, SMALL)]], dtype=f32)
    got_small = swap_chip(small)
    own_rows, returned = finish(mine, other_rows, every, vectors, tie(grad_middle, attn_kept, small))
    returned = swap_chip(returned)
    (small,) = fold(small, tie(got_small, own_rows), [[(0, SMALL)]], dtype=f32)
    def settle(kept, got_kept, returned):
        kept = join(kept, got_kept, bits[0], spot)
        returned = returned.astype(f32)
        grad_frames = jnp.where(
            chip == 0, jnp.stack([own_rows, returned]), jnp.stack([returned, own_rows])
        )
        kept = kept.astype(f32)
        grad_out = kept[:share]
        grad_up = kept[share : share + deep]
        grad_down = kept[share + deep : block]
        head_mine = kept[block : block + half]
        head_other = swap_core(head_mine.astype(bf16)).astype(f32)
        grad_head = jnp.where(
            core == 0,
            jnp.concatenate([head_mine, head_other], axis=0),
            jnp.concatenate([head_other, head_mine], axis=0),
        )
        second_set = update(out_proj, momentum_out, average_out, grad_out)
        third_set = update(up_proj, momentum_up, average_up, grad_up)
        fifth_set = update(down_proj, momentum_down, average_down, grad_down)
        sixth_set = update(head_proj, momentum_head, average_head, grad_head)
        return grad_frames, *second_set, *third_set, *fifth_set, *sixth_set

    for step in steps:
        got_small = swap_dp(small, step, size)
        if step == steps[-1]:
            last = settle(kept, got_kept, returned)
            got_attn = tie(got_attn, *last)
        (attn_kept,) = fold(
            attn_kept, tie(got_attn, small), [[(0, rows)]], dtype=f32 if step == steps[-1] else bf16
        )
        if step < steps[-1]:
            got_attn = swap_dp(attn_kept, 2 * step, size)
        (small,) = fold(small, tie(got_small, attn_kept), [[(0, SMALL)]], dtype=f32)
        if step == 1:
            for high in steps[2:]:
                got_step = tie(got_step, small) if high == steps[2] else swap_dp(kept, high, size)
                (kept,) = fold(kept, got_step, [[(0, full // 2)]])
            got_kept = swap_dp(kept, 1, size)
        elif step == 2:
            returned = tie(returned, attn_kept)
    grad_frames, *sets = last
    second_set, third_set, fifth_set, sixth_set = (sets[k : k + 3] for k in range(0, 12, 3))
    grad_attn_proj = jnp.swapaxes(attn_kept.reshape(3, share, HEAD), 1, 2)
    loss = small[7, 0]
    grad_up_bias = pick(small[8:12], place)
    grad_vectors = jnp.concatenate([small[12:14], small[:7]], axis=0)
    first_set = update(attn_proj, momentum_attn, average_attn, grad_attn_proj)
    fourth_set = update(up_bias, momentum_bias, average_bias, grad_up_bias)
    seventh_set = update(vectors, momentum_vectors, average_vectors, grad_vectors)
    return (
        loss,
        first_set[0],
        second_set[0],
        third_set[0],
        fourth_set[0],
        fifth_set[0],
        sixth_set[0],
        seventh_set[0],
        first_set[1],
        second_set[1],
        third_set[1],
        fourth_set[1],
        fifth_set[1],
        sixth_set[1],
        seventh_set[1],
        first_set[2],
        second_set[2],
        third_set[2],
        fourth_set[2],
        fifth_set[2],
        sixth_set[2],
        seventh_set[2],
        grad_frames,
    )


def solution(mesh):
    in_specs = (
        P("dp", "tp", None),
        P("dp", "tp", None),
        P("dp", None),
        P("dp", None),
        P(None, None, "tp"),
        P("tp", None),
        P(None, "tp"),
        P("tp"),
        P(None, "tp"),
        P(),
        P(),
        P(None, None, "tp"),
        P("tp", None),
        P(None, "tp"),
        P("tp"),
        P(None, "tp"),
        P(),
        P(),
        P(None, None, "tp"),
        P("tp", None),
        P(None, "tp"),
        P("tp"),
        P(None, "tp"),
        P(),
        P(),
    )
    out_specs = (
        P(),
        P(None, None, "tp"),
        P("tp", None),
        P(None, "tp"),
        P("tp"),
        P(None, "tp"),
        P(),
        P(),
        P(None, None, "tp"),
        P("tp", None),
        P(None, "tp"),
        P("tp"),
        P(None, "tp"),
        P(),
        P(),
        P(None, None, "tp"),
        P("tp", None),
        P(None, "tp"),
        P("tp"),
        P(None, "tp"),
        P(),
        P(),
        P("dp", "tp", None),
    )
    return jax.shard_map(
        per_device, mesh=mesh, in_specs=in_specs, out_specs=out_specs, check_vma=False
    )
```

```python
import functools
import math

import jax
import jax.numpy as jnp
from jax import lax
from jax.experimental import pallas as pl
from jax.experimental.pallas import tpu as pltpu
from jax.sharding import PartitionSpec as P

CHN = 96
HDIM = 48
HPAD = 64
HEAD = 384


EPSILON = 1e-05
MOMENTUM_RATE = 0.9
LEARN_RATE = 0.02
AVERAGE_RATE = 0.9
SCALE = HDIM ** (-0.5)
LOG_SCALE = SCALE * math.log2(math.e)
GELU_A = math.sqrt(2.0 / math.pi)
GELU_B = 0.044715
SMALL = 16
BLOCK = 384
ROWS = 64
CHUNKS = 3

bf16 = jnp.bfloat16
f32 = jnp.float32
HBM = pl.BlockSpec(memory_space=pltpu.HBM)
SMEM = pl.BlockSpec(memory_space=pltpu.SMEM)
VMEM = pl.BlockSpec(memory_space=pltpu.VMEM)


def kernel_call(body, outs, inputs, limit, micros, name, in_specs=None, out_specs=None, scratch=(), aliases=None):
    return pl.pallas_call(
        body,
        out_shape=outs,
        in_specs=in_specs or [VMEM] * len(inputs),
        out_specs=out_specs or jax.tree.map(lambda _: VMEM, outs),
        scratch_shapes=list(scratch),
        input_output_aliases=aliases or {},
        compiler_params=pltpu.CompilerParams(vmem_limit_bytes=limit << 20),
        cost_estimate=pl.CostEstimate(flops=int(micros * 1e9), bytes_accessed=0, transcendentals=0),
        name=name,
    )(*inputs)


def struct(rows, columns, dtype):
    return jax.ShapeDtypeStruct((rows, columns), dtype)


def contract(left, right, left_dim, right_dim):
    return lax.dot_general(
        left, right, (((left_dim,), (right_dim,)), ((), ())), preferred_element_type=f32
    )


def row_mean(values):
    return jnp.mean(values, axis=-1, keepdims=True)


def column_sum(values):
    return jnp.sum(values, axis=0, keepdims=True)


def normalise(values):
    centred = values - row_mean(values)
    inverse = lax.rsqrt(row_mean(centred * centred) + EPSILON)
    return centred * inverse, inverse


def aligned(index, size):
    return pl.ds(pl.multiple_of(index * size, size), size)


def forward_body(first, heads, query, key, value, *refs):
    mixed, totals, weights, slots, sems = refs[-5:]

    def out_copy(h):
        slot = lax.rem(h, 2)
        return pltpu.make_async_copy(slots.at[slot], weights.at[h + first], sems.at[slot])

    def head(h, carry):
        @pl.when(h >= 2)
        def _():
            out_copy(h - 2).wait()

        rows = aligned(h, HDIM)
        scores = contract(query[rows], key[rows], 0, 0)
        maximum = jnp.max(scores, axis=1, keepdims=True)
        exponent = jnp.exp2((scores - maximum) * LOG_SCALE).astype(bf16)
        slots[lax.rem(h, 2)] = exponent
        out_copy(h).start()
        summed = contract(value[aligned(h, HPAD)], exponent, 1, 1)
        total = summed[HDIM : HDIM + 1]
        mixed[rows] = (summed[:HDIM] / total).astype(bf16)
        totals[pl.ds(h, 1)] = total
        return carry

    lax.fori_loop(0, heads, head, 0)
    for h in range(max(0, heads - 2), heads):
        out_copy(h).wait()


def attention_forward(query, key, value, weights=None):
    heads = query.shape[0] // HDIM
    first = 0 if weights is None else heads
    rows, length = query.shape[1], key.shape[1]
    return kernel_call(
        functools.partial(forward_body, first, heads),
        [
            struct(heads * HDIM, rows, bf16),
            struct(heads, rows, f32),
            jax.ShapeDtypeStruct((2 * heads, rows, length), bf16),
        ],
        (query, key, value) if weights is None else (query, key, value, weights),
        FORWARD_LIMIT,
        4 * heads,
        "attention_forward",
        in_specs=[VMEM] * 3 if weights is None else [VMEM] * 3 + [HBM],
        aliases={} if weights is None else {3: 2},
        out_specs=[VMEM, VMEM, HBM],
        scratch=[pltpu.VMEM((2, rows, length), bf16), pltpu.SemaphoreType.DMA((2,))],
    )


def backward_body(
    first, base, heads, query, key, value, mixed, grad_mixed, totals, weights,
    grad_query, grad_key, grad_value, slots, sums, scaled_all, sems
):
    def in_copy(h):
        slot = lax.rem(h, 2)
        return pltpu.make_async_copy(weights.at[h + base], slots.at[slot], sems.at[slot])

    in_copy(0).start()
    width = key.shape[1] // CHUNKS

    def head(h, carry):
        @pl.when(h + 1 < heads)
        def _():
            in_copy(h + 1).start()

        rows, here = aligned(h + first, HDIM), aligned(h, HDIM)
        inverse = 1.0 / totals[pl.ds(h + first, 1)]
        grad = grad_mixed[rows].astype(f32)
        delta = column_sum(grad * mixed[rows].astype(f32))
        scaled = (grad * inverse).astype(bf16)
        offset = -delta * inverse
        high = offset.astype(bf16).astype(f32)
        row = lax.broadcasted_iota(jnp.int32, (HPAD - HDIM, offset.shape[1]), 0)
        extra = jnp.where(row == 0, high, jnp.where(row == 1, offset - high, 0.0)).astype(bf16)
        scaled_all[...] = jnp.concatenate([scaled, extra], axis=0)
        sums[...] = jnp.zeros_like(sums)
        in_copy(h).wait()

        def chunk(i, carry):
            part = aligned(i, width)
            grad_weights = contract(scaled_all[...], value[aligned(h + first, HPAD), part], 0, 0)
            kept = slots[lax.rem(h, 2), :, part]
            grad_scores = (kept.astype(f32) * grad_weights).astype(bf16)
            sums[...] += contract(key[rows, part], grad_scores, 1, 1)
            grad_key[here, part] = (contract(query[rows], grad_scores, 1, 0) * SCALE).astype(bf16)
            grad_value[here, part] = contract(scaled_all[:HDIM], kept, 1, 0).astype(bf16)
            return carry

        lax.fori_loop(0, CHUNKS, chunk, 0)
        grad_query[here] = (sums[...] * SCALE).astype(bf16)
        return carry

    lax.fori_loop(0, heads, head, 0)


def attention_backward(first, base, heads, query, key, value, mixed, grad_mixed, totals, weights):
    rows, length = query.shape[1], key.shape[1]
    return kernel_call(
        functools.partial(backward_body, first, base, heads),
        [
            struct(heads * HDIM, rows, bf16),
            struct(heads * HDIM, length, bf16),
            struct(heads * HDIM, length, bf16),
        ],
        (query, key, value, mixed, grad_mixed, totals, weights),
        BACKWARD_LIMIT,
        5.5 * heads,
        "attention_backward",
        in_specs=[VMEM] * 6 + [HBM],
        scratch=[
            pltpu.VMEM((2, rows, length), bf16),
            pltpu.VMEM((HDIM, rows), f32),
            pltpu.VMEM((HPAD, rows), bf16),
            pltpu.SemaphoreType.DMA((2,)),
        ],
    )


def take_body(place, stacked, taken):
    taken[...] = stacked[place[0]]


def take(stacked, place):
    count, rows, columns = stacked.shape
    return kernel_call(
        take_body, struct(rows, columns, stacked.dtype), (place, stacked), 2, 1, "take", in_specs=[SMEM, VMEM]
    )


def pack_body(place, attn, out, up, down, bias, targets, attn_low, sent, goal):
    share, deep = out.shape[0], up.shape[0]
    base = share + 2 * deep
    goal[...] = targets[place[0]]
    attn_low[...] = attn[...].astype(bf16)
    sent[:share] = out[...].astype(bf16)
    sent[share : share + deep] = up[...].astype(bf16)
    sent[share + deep : base] = down[...].astype(bf16)
    high = bias[...].astype(bf16)
    low = (bias[...] - high.astype(f32)).astype(bf16)
    zeros = jnp.zeros((SMALL - 2, bias.shape[1]), bf16)
    sent[base : base + SMALL] = jnp.concatenate([high, low, zeros], axis=0)


def pack(place, attn, out, up, down, bias, targets):
    rows = out.shape[0] + 2 * up.shape[0] + SMALL
    return kernel_call(
        pack_body,
        [struct(attn.shape[0], HEAD, bf16), struct(rows, HEAD, bf16), struct(targets.shape[1], HEAD, bf16)],
        (place, attn, out, up, down, bias, targets),
        8,
        PACK_MICROS,
        "pack",
        in_specs=[SMEM] + [VMEM] * 6,
    )


def weight_rows(left, right):
    share = left.shape[0] // 3
    return jnp.concatenate(
        [block[m * share : (m + 1) * share] for m in range(3) for block in (left, right)], axis=0
    )


def project_into(normed, left, right, query, key, value):
    weights = weight_rows(left[...], right[...])
    size = weights.shape[0] // 3
    rows = query.shape[1]
    query[...] = contract(weights[:size], normed[:rows], 1, 1).astype(bf16)
    both = contract(weights[size:], normed, 1, 1).astype(bf16)
    key[...] = both[:size]
    row = lax.broadcasted_iota(jnp.int32, (HPAD - HDIM, normed.shape[0]), 0)
    ends = jnp.where(row < 2, 1.0, 0.0).astype(bf16)
    for h in range(size // HDIM):
        value[h * HPAD : h * HPAD + HDIM] = both[size + h * HDIM : size + (h + 1) * HDIM]
        value[h * HPAD + HDIM : (h + 1) * HPAD] = ends


def project_near_body(
    place, frames, got, frames_other, got_other, vectors, left, right, query, key, value, first, every
):
    quarter = got.shape[0]
    for j, source in enumerate((frames, got, frames_other, got_other)):
        part = source[place[0]] if j % 2 == 0 else source[...]
        rows = slice(j * quarter, (j + 1) * quarter)
        every[rows] = part
        first[rows] = (normalise(part.astype(f32))[0] * vectors[0:1] + vectors[1:2]).astype(bf16)
    project_into(first[...], left, right, query, key, value)


def projected(rows, length, size):
    return [
        struct(size, rows, bf16),
        struct(size, length, bf16),
        struct(size // HDIM * HPAD, length, bf16),
    ]


def project_near(place, frames, got, frames_other, got_other, vectors, left, right):
    quarter, model = got.shape
    size = 2 * left.shape[0] // 3
    return kernel_call(
        project_near_body,
        projected(2 * quarter, 4 * quarter, size) + [struct(4 * quarter, model, bf16)] * 2,
        (place, frames, got, frames_other, got_other, vectors, left, right),
        16,
        4,
        "project_near",
        in_specs=[SMEM] + [VMEM] * 7,
    )


def project_far_body(first, *refs):
    project_into(first[...], *refs)


def project_far(first, left, right):
    length = first.shape[0]
    size = 2 * left.shape[0] // 3
    return kernel_call(
        project_far_body,
        projected(length // 2, length, size),
        (first, left, right),
        12,
        3,
        "project_far",
    )


def by_rows(function, *values):
    pieces = [
        function(*(v[start : start + ROWS] for v in values)) for start in range(0, values[0].shape[0], ROWS)
    ]
    return [jnp.concatenate(parts, axis=0) for parts in zip(*pieces)]


def middle_body(
    place, attended_near, attended_far, frames, targets, goal_got, keep, vectors, head, *refs
):
    blocks = refs[:4]
    grad_middle_out, grad_near, grad_far, kept_out, sent_out, small_out = refs[4:10]
    second_all, ffn_all, final_all, pred_all, attn_all, hidden_all, pre_all, goal, bias_sums = refs[10:]
    rows = grad_middle_out.shape[0]
    quarter = targets.shape[1]
    deep = head.shape[0]
    share = grad_near.shape[0] // 2
    base = share + 2 * deep
    half = 2 * share
    goal[:quarter] = targets[place[1]]
    goal[quarter:] = goal_got[...]
    gain, shift = vectors[4:5], vectors[5:6]
    scale_one, scale_two = vectors[3:4], vectors[7:8]
    out_low = jnp.concatenate([b[:share] for b in blocks], axis=0)
    head_low = head[...].astype(bf16)
    small_out[...] = jnp.zeros_like(small_out)
    bias_sums[...] = jnp.zeros_like(bias_sums)

    def block_step(step, carry):
        here = aligned(step, BLOCK)

        def add(row, values):
            small_out[row : row + 1] += column_sum(values)

        mixed = contract(attended_near[:, here], out_low[:half], 0, 0) + contract(
            attended_far[:, here], out_low[half:], 0, 0
        )

        def first_norm(mixed, frames):
            biased = mixed + vectors[2:3]
            middle = frames.astype(f32) + scale_one * biased
            normed, inverse = normalise(middle)
            return biased, middle, normed, inverse, (normed * gain + shift).astype(bf16)

        biased_one, middle, normed, inverse, second = by_rows(first_norm, mixed, frames[here])
        second_all[here] = second
        slopes = []
        mixed = None
        for j, block in enumerate(blocks):
            parts = block[base : base + SMALL].astype(f32)
            bias = parts[0:1] + parts[1:2]

            def gelu(pre):
                pre = pre + bias
                square = pre * pre
                tanh = jnp.tanh(pre * (GELU_A + (GELU_A * GELU_B) * square))
                phi = 0.5 + 0.5 * tanh
                curve = (1.0 - tanh * tanh) * (0.5 * GELU_A + (1.5 * GELU_A * GELU_B) * square)
                return (pre * phi).astype(bf16), phi + pre * curve

            hidden, slope = by_rows(gelu, contract(second, block[share : share + deep], 1, 0))
            hidden_all[j, here] = hidden
            slopes.append(slope)
            part = contract(hidden, block[share + deep : base], 1, 1)
            mixed = part if j == 0 else mixed + part

        def second_scale(mixed, middle):
            biased = mixed + vectors[6:7]
            return biased, (middle + scale_two * biased).astype(bf16)

        biased_two, final = by_rows(second_scale, mixed, middle)
        final_all[here] = final

        def error(pred, goal):
            diff = pred + vectors[8:9] - goal.astype(f32)
            smooth = jnp.sqrt(diff * diff + 1.0)
            add(7, keep[...] * (smooth - 1.0) / HEAD)
            grad = (keep[...] * (diff / smooth) / HEAD).astype(bf16)
            add(6, grad.astype(f32))
            return (grad,)

        (grad_pred,) = by_rows(error, contract(final, head_low, 1, 0), goal[here])
        pred_all[here] = grad_pred

        grad_final = contract(grad_pred, head_low, 1, 1)

        def scale_back(grad, biased):
            ffn = grad * scale_two
            add(4, ffn)
            add(5, grad * biased)
            return (ffn.astype(bf16),)

        (ffn_low,) = by_rows(scale_back, grad_final, biased_two)
        ffn_all[here] = ffn_low
        grad_second = None
        for j, block in enumerate(blocks):

            def gelu_back(grad, slope):
                low = (grad * slope).astype(bf16)
                bias_sums[j : j + 1] += column_sum(low.astype(f32))
                return (low,)

            grad = contract(ffn_low, block[share + deep : base], 1, 0)
            (low,) = by_rows(gelu_back, grad, slopes[j])
            pre_all[j, here] = low
            part = contract(low, block[share : share + deep], 1, 1)
            grad_second = part if j == 0 else grad_second + part

        def norm_back(grad, normed, inverse, grad_final, biased):
            add(2, grad * normed)
            add(3, grad)
            scaled = grad * gain
            back = inverse * (scaled - row_mean(scaled) - normed * row_mean(scaled * normed))
            total = grad_final + back
            attn = total * scale_one
            add(0, attn)
            add(1, total * biased)
            return total, attn.astype(bf16)

        grad_middle, attn_low = by_rows(norm_back, grad_second, normed, inverse, grad_final, biased_one)
        grad_middle_out[here] = grad_middle
        attn_all[here] = attn_low
        grad_near[:, here] = contract(out_low[:half], attn_low, 1, 1).astype(bf16)
        grad_far[:, here] = contract(out_low[half:], attn_low, 1, 1).astype(bf16)
        return carry

    lax.fori_loop(0, rows // BLOCK, block_step, 0)

    attn_low = attn_all[...]
    grad_out = jnp.concatenate(
        [contract(attended_near[...], attn_low, 1, 0), contract(attended_far[...], attn_low, 1, 0)], axis=0
    ).astype(bf16)
    for j in range(4):
        target = (kept_out, sent_out)[j % 2]
        start = (j // 2) * base
        target[start : start + share] = grad_out[j * share : (j + 1) * share]
        small_out[pl.ds(8 + lax.bitwise_xor(place[0], j), 1)] = bias_sums[j : j + 1]

    def weight_step(i, carry):
        for k, target in enumerate((kept_out, sent_out)):
            start = pl.multiple_of(i * base + share, SMALL)
            up = contract(second_all[...], pre_all[2 * i + k], 0, 0).astype(bf16)
            down = contract(ffn_all[...], hidden_all[2 * i + k], 0, 0).astype(bf16)
            target[pl.ds(start, deep)] = up
            target[pl.ds(pl.multiple_of(start + deep, SMALL), deep)] = down
        return carry

    lax.fori_loop(0, 2, weight_step, 0)
    grad_head = contract(final_all[...], pred_all[...], 0, 0).astype(bf16)
    column = lax.broadcasted_iota(jnp.int32, (1, HEAD), 1)
    loss = jnp.sum(small_out[7:8], axis=1, keepdims=True)
    small_out[7:8] = jnp.where(column == 0, loss, 0.0)
    core = lax.rem(place[0], 2)
    size = deep // 2
    for target, first in ((kept_out, core == 0), (sent_out, core == 1)):
        target[2 * base : 2 * base + size] = jnp.where(first, grad_head[:size], grad_head[size:])
        target[2 * base + size :] = jnp.zeros((2 * SMALL, HEAD), bf16)


def middle_step(place, attended_near, attended_far, frames, targets, goal_got, keep, vectors, head, blocks):
    rows, model = frames.shape[0] // 2, frames.shape[1]
    base = blocks[0].shape[0] - SMALL
    count = 2 * base + HEAD // 2 + 2 * SMALL
    inputs = (place, attended_near, attended_far, frames, targets, goal_got, keep, vectors, head, *blocks)
    return kernel_call(
        middle_body,
        [
            struct(rows, model, f32),
            struct(*attended_near.shape, bf16),
            struct(*attended_far.shape, bf16),
            struct(count, HEAD, bf16),
            struct(count, HEAD, bf16),
            struct(SMALL, HEAD, f32),
        ],
        inputs,
        MIDDLE_LIMIT,
        20,
        "middle_step",
        in_specs=[SMEM] + [VMEM] * 12,
        scratch=[
            *[pltpu.VMEM((rows, model), bf16)] * 5,
            pltpu.VMEM((4, rows, HEAD), bf16),
            pltpu.VMEM((4, rows, HEAD), bf16),
            pltpu.VMEM((rows, HEAD), bf16),
            pltpu.VMEM((8, HEAD), f32),
        ],
    )


def fold_body(plan, place, left, right, *targets):
    for target, ranges in zip(targets, plan):
        base = 0
        for start, stop, *choice in ranges:
            if choice:
                size = (stop - start) // 2
                source = pl.ds(pl.multiple_of(start + choice[0](place) * size, SMALL), size)
            else:
                size = stop - start
                source = pl.ds(start, size)
            total = left[source].astype(f32) + right[source].astype(f32)
            target[base : base + size] = total.astype(target.dtype)
            base += size


def fold(left, right, plan, place=None, dtype=bf16):
    shapes = [
        struct(sum((r[1] - r[0]) // (2 if len(r) > 2 else 1) for r in ranges), left.shape[1], dtype)
        for ranges in plan
    ]
    if place is None:
        place = jnp.zeros((1,), jnp.int32)
    return kernel_call(
        functools.partial(fold_body, plan),
        shapes,
        (place, left, right),
        6,
        0.3,
        "fold",
        in_specs=[SMEM, VMEM, VMEM],
    )


def join_body(bit, place, kept, got, both):
    size = kept.shape[0]
    both[pl.ds(pl.multiple_of(bit(place) * size, SMALL), size)] = kept[...]
    both[pl.ds(pl.multiple_of((1 - bit(place)) * size, SMALL), size)] = got[...]


def join(kept, got, bit, place):
    return kernel_call(
        functools.partial(join_body, bit),
        struct(2 * kept.shape[0], kept.shape[1], kept.dtype),
        (place, kept, got),
        6,
        0.3,
        "join",
        in_specs=[SMEM, VMEM, VMEM],
    )


def gather_rows(parts):
    return jnp.concatenate([p[...] for p in parts], axis=0)


def weight_grads(grads, first, kept, sent, base=0):
    queries, keys, values = grads
    rows = queries[0].shape[1]
    query = contract(gather_rows(queries), first[:rows], 1, 0)
    both = contract(gather_rows(keys + values), first[...], 1, 0)
    share = query.shape[0] // 2
    for m in range(3):
        for j, target in enumerate((kept, sent)):
            start = (max(m - 1, 0) * 2 + j) * share
            part = (query if m == 0 else both)[start : start + share]
            target[m * share : (m + 1) * share] = part.astype(bf16)


def far_grads_body(calls, first, *refs):
    grads = [refs[k * calls : (k + 1) * calls] for k in range(3)]
    weight_grads(grads, first[...], *refs[3 * calls :])


def far_grads(grads, first):
    queries, keys, values = zip(*grads)
    count = 3 * sum(q.shape[0] for q in queries) // 2
    return kernel_call(
        functools.partial(far_grads_body, len(grads)),
        [struct(count, HEAD, bf16)] * 2,
        (first, *queries, *keys, *values),
        12,
        4,
        "far_grads",
    )


def post_body(calls, near, *refs):
    queries, keys, values = (refs[k * calls : (k + 1) * calls] for k in range(3))
    first, frames, vectors, small_in = refs[3 * calls : 3 * calls + 4]
    blocks = refs[3 * calls + 4 : 3 * calls + 8]
    mine, other, kept, sent, small = refs[3 * calls + 8 :]
    share = blocks[0].shape[0] // 3
    rows = mine.shape[0]

    def rows_of(m):
        return jnp.concatenate([b[m * share : (m + 1) * share] for b in blocks], axis=0)

    weight_grads((queries[:near], keys[:near], values[:near]), first[...], kept, sent)
    both = jnp.concatenate([rows_of(1), rows_of(2)], axis=0)
    query_rows = rows_of(0)
    small[...] = small_in[...]

    def part(step, carry):
        here = aligned(step, BLOCK)
        there = pl.ds(pl.multiple_of(rows + step * BLOCK, BLOCK), BLOCK)

        def pulled(parts, columns, weights):
            return contract(jnp.concatenate([p[:, columns] for p in parts], axis=0), weights, 0, 0)

        def ends(total, place):
            normed = normalise(frames[place].astype(f32))[0]
            small[12:13] += column_sum(total * normed)
            small[13:14] += column_sum(total)

        total = pulled(keys + values, here, both) + pulled(queries, here, query_rows)
        mine[here] = total
        ends(total, here)
        rest = pulled(keys + values, there, both)
        other[here] = rest.astype(bf16)
        ends(rest, there)
        return carry

    lax.fori_loop(0, rows // BLOCK, part, 0)


def post_step(grads, first, frames, vectors, small, blocks):
    length, model = first.shape
    rows = length // 2
    queries, keys, values = zip(*grads)
    payload = struct(blocks[0].shape[0], model, bf16)
    return kernel_call(
        functools.partial(post_body, len(grads), 2),
        [struct(rows, model, f32), struct(rows, model, bf16), payload, payload, struct(*small.shape, f32)],
        (*queries, *keys, *values, first, frames, vectors, small, *blocks),
        POST_LIMIT,
        8,
        "post_step",
    )


def finish_body(mine, got, frames, vectors, grad_middle, own, returned):
    quarter = own.shape[0]
    size = quarter // 3

    def part(step, carry):
        for target, base in ((own, 0), (returned, quarter)):
            there = aligned(step, size)
            here = pl.ds(pl.multiple_of(base + step * size, size), size)
            grad = mine[here] + got[here].astype(f32)
            normed, inverse = normalise(frames[here].astype(f32))
            scaled = grad * vectors[0:1]
            back = inverse * (scaled - row_mean(scaled) - normed * row_mean(scaled * normed))
            target[there] = (grad_middle[here] + back).astype(target.dtype)
        return carry

    lax.fori_loop(0, 3, part, 0)


def finish(mine, got, frames, vectors, grad_middle):
    rows, model = mine.shape
    return kernel_call(
        finish_body,
        [struct(rows // 2, model, f32), struct(rows // 2, model, bf16)],
        (mine, got, frames, vectors, grad_middle),
        16,
        3,
        "finish",
    )


def update(weight, moment, average, grad):
    moment_new = MOMENTUM_RATE * moment + grad
    weight_new = weight - LEARN_RATE * (grad + MOMENTUM_RATE * moment_new)
    average_new = AVERAGE_RATE * average + (1.0 - AVERAGE_RATE) * weight_new
    return (weight_new, moment_new, average_new)


CORE_PAIRS = [(0, 1), (1, 0), (2, 3), (3, 2)]
CHIP_PAIRS = [(0, 2), (2, 0), (1, 3), (3, 1)]
FORWARD_LIMIT = 28
BACKWARD_LIMIT = 28
MIDDLE_LIMIT = 30
POST_LIMIT = 20
PACK_MICROS = 3


def swap_core(values):
    return lax.ppermute(values, "tp", CORE_PAIRS)


def swap_chip(values):
    return lax.ppermute(values, "tp", CHIP_PAIRS)


def swap_dp(values, step, size):
    return lax.ppermute(values, "dp", [(i, i ^ step) for i in range(size)])


def pick(stacked, place):
    return lax.dynamic_index_in_dim(stacked, place, 0, False)


def tie(value, *others):
    return lax.optimization_barrier((value, *others))[0]


def per_device(
    frames,
    targets,
    presence,
    order,
    attn_proj,
    out_proj,
    up_proj,
    up_bias,
    down_proj,
    head_proj,
    vectors,
    momentum_attn,
    momentum_out,
    momentum_up,
    momentum_bias,
    momentum_down,
    momentum_head,
    momentum_vectors,
    average_attn,
    average_out,
    average_up,
    average_bias,
    average_down,
    average_head,
    average_vectors,
):
    size = lax.axis_size("dp")
    place = lax.axis_index("tp")
    chip, core = place // 2, place % 2
    share, deep = out_proj.shape[0], up_proj.shape[0]
    got = swap_chip(take(frames, (1 - chip).reshape(1)))
    frames_other = swap_core(frames)
    attn_own, sent, goal = pack(
        order[0, 1 - chip].reshape(1),
        jnp.swapaxes(attn_proj, 1, 2).reshape(3 * share, HEAD),
        out_proj,
        up_proj,
        down_proj,
        up_bias[None],
        targets,
    )
    attn_core = swap_core(attn_own)
    sent_core = swap_core(sent)
    got_other = swap_core(tie(got, attn_own))
    attn_chip = swap_chip(tie(attn_own, got))
    query, key, value, first, every = project_near(
        chip.reshape(1), frames, got, frames_other, got_other, vectors, attn_own, attn_core
    )
    sent_chip = swap_chip(tie(sent, first))
    near = (query, key, value)
    near_out = attention_forward(*near)
    attn_both = swap_core(tie(attn_chip, first))
    far = project_far(tie(first, near_out[0]), attn_chip, attn_both)
    sent_both = swap_core(tie(sent_chip, far[0]))
    goal_got = swap_chip(tie(goal, far[0]))
    far_out = attention_forward(*far, near_out[2])
    keep = jnp.repeat(pick(presence, chip).astype(f32), CHN)[None, :]
    where = jnp.stack([place, order[0, chip]])
    grad_middle, grad_near, grad_far, kept, sent, small = middle_step(
        where, near_out[0], far_out[0], every, targets, goal_got, keep, vectors, head_proj,
        (sent, sent_core, sent_chip, sent_both),
    )

    inputs = ((*near, near_out[0], grad_near, near_out[1], far_out[2]), (*far, far_out[0], grad_far, *far_out[1:]))
    here = near[0].shape[0] // HDIM

    def backward(part, first_head, heads, *after):
        query, *others = inputs[part]
        return attention_backward(first_head, part * here + first_head, heads, tie(query, *after), *others)

    block = share + 2 * deep
    half = HEAD // 2
    full = block + half + 2 * SMALL
    spot = lax.axis_index("dp").reshape(1)
    bits = [lambda p: p[0] % 2, lambda p: p[0] // 2 % 2]
    others = [lambda p: 1 - p[0] % 2, lambda p: 1 - p[0] // 2 % 2]
    steps = [1 << k for k in range(size.bit_length() - 1)]
    last_rows = (2 * block, full + block)
    rows = 3 * share

    got_core = swap_core(sent)
    kept, sent = fold(
        kept, got_core, [[(0, block), last_rows], [(block, 2 * block), last_rows]]
    )
    got_chip = swap_chip(sent)
    far_all = backward(1, 0, here, sent)
    kept, sent = fold(
        kept, tie(got_chip, far_all[0]), [[(0, full, bits[0])], [(0, full, others[0])]], spot
    )
    got_y = swap_dp(sent, 1, size)
    far_kept, far_sent = far_grads([far_all], tie(first, sent))
    got_far = swap_core(far_sent)
    near_one = backward(0, 0, here // 2, sent, far_sent)
    (far_kept,) = fold(far_kept, tie(got_far, near_one[0]), [[(0, rows)]])
    got_far = swap_chip(far_kept)
    kept, sent = fold(
        kept, tie(got_y, near_one[0]), [[(0, full // 2, bits[1])], [(0, full // 2, others[1])]], spot
    )
    got_z = swap_dp(sent, 2, size)
    near_two = backward(0, here // 2, here // 2, sent, far_kept)
    (kept,) = fold(kept, tie(got_z, near_two[0]), [[(0, full // 4)]])
    got_step = swap_dp(kept, steps[2], size)
    mine, other, near_kept, near_sent, small = post_step(
        [near_one, near_two, far_all],
        tie(first, kept, got_far),
        every,
        vectors,
        small,
        (attn_own, attn_core, attn_chip, attn_both),
    )
    got_near = swap_core(near_sent)
    got_small = swap_core(small)
    other_rows = swap_core(other)
    (near_kept,) = fold(near_kept, got_far, [[(0, rows)]], dtype=f32)
    (attn_kept,) = fold(near_kept, got_near, [[(0, rows)]])
    got_attn = swap_dp(attn_kept, 1, size)
    (small,) = fold(small, tie(got_small, attn_kept), [[(0, SMALL)]], dtype=f32)
    got_small = swap_chip(small)
    own_rows, returned = finish(mine, other_rows, every, vectors, tie(grad_middle, attn_kept, small))
    (small,) = fold(small, tie(got_small, own_rows), [[(0, SMALL)]], dtype=f32)
    returned = swap_chip(tie(returned, small))
    def settle(kept, got_kept, returned):
        kept = join(kept, got_kept, bits[0], spot)
        returned = returned.astype(f32)
        grad_frames = jnp.where(
            chip == 0, jnp.stack([own_rows, returned]), jnp.stack([returned, own_rows])
        )
        kept = kept.astype(f32)
        grad_out = kept[:share]
        grad_up = kept[share : share + deep]
        grad_down = kept[share + deep : block]
        head_mine = kept[block : block + half]
        head_other = swap_core(head_mine.astype(bf16)).astype(f32)
        grad_head = jnp.where(
            core == 0,
            jnp.concatenate([head_mine, head_other], axis=0),
            jnp.concatenate([head_other, head_mine], axis=0),
        )
        second_set = update(out_proj, momentum_out, average_out, grad_out)
        third_set = update(up_proj, momentum_up, average_up, grad_up)
        fifth_set = update(down_proj, momentum_down, average_down, grad_down)
        sixth_set = update(head_proj, momentum_head, average_head, grad_head)
        return grad_frames, *second_set, *third_set, *fifth_set, *sixth_set

    for step in steps:
        got_small = swap_dp(small, step, size)
        if step == steps[-1]:
            last = settle(kept, got_kept, returned)
            got_attn = tie(got_attn, last[0])
        (attn_kept,) = fold(
            attn_kept, tie(got_attn, small), [[(0, rows)]], dtype=f32 if step == steps[-1] else bf16
        )
        if step < steps[-1]:
            got_attn = swap_dp(attn_kept, 2 * step, size)
        if step == 2:
            kept = join(kept, tie(got_kept, attn_kept), bits[1], spot)
            got_kept = swap_dp(kept, 1, size)
            got_small = tie(got_small, kept)
        (small,) = fold(small, tie(got_small, attn_kept), [[(0, SMALL)]], dtype=f32)
        if step == 1:
            for high in steps[2:]:
                got_step = tie(got_step, small) if high == steps[2] else swap_dp(kept, high, size)
                (kept,) = fold(kept, got_step, [[(0, full // 4)]])
            got_kept = swap_dp(kept, 2, size)
        elif step == 2:
            returned = tie(returned, attn_kept)
    grad_frames, *sets = last
    second_set, third_set, fifth_set, sixth_set = (sets[k : k + 3] for k in range(0, 12, 3))
    grad_attn_proj = jnp.swapaxes(attn_kept.reshape(3, share, HEAD), 1, 2)
    loss = small[7, 0]
    grad_up_bias = pick(small[8:12], place)
    grad_vectors = jnp.concatenate([small[12:14], small[:7]], axis=0)
    first_set = update(attn_proj, momentum_attn, average_attn, grad_attn_proj)
    fourth_set = update(up_bias, momentum_bias, average_bias, grad_up_bias)
    seventh_set = update(vectors, momentum_vectors, average_vectors, grad_vectors)
    return (
        loss,
        first_set[0],
        second_set[0],
        third_set[0],
        fourth_set[0],
        fifth_set[0],
        sixth_set[0],
        seventh_set[0],
        first_set[1],
        second_set[1],
        third_set[1],
        fourth_set[1],
        fifth_set[1],
        sixth_set[1],
        seventh_set[1],
        first_set[2],
        second_set[2],
        third_set[2],
        fourth_set[2],
        fifth_set[2],
        sixth_set[2],
        seventh_set[2],
        grad_frames,
    )


def solution(mesh):
    in_specs = (
        P("dp", "tp", None),
        P("dp", "tp", None),
        P("dp", None),
        P("dp", None),
        P(None, None, "tp"),
        P("tp", None),
        P(None, "tp"),
        P("tp"),
        P(None, "tp"),
        P(),
        P(),
        P(None, None, "tp"),
        P("tp", None),
        P(None, "tp"),
        P("tp"),
        P(None, "tp"),
        P(),
        P(),
        P(None, None, "tp"),
        P("tp", None),
        P(None, "tp"),
        P("tp"),
        P(None, "tp"),
        P(),
        P(),
    )
    out_specs = (
        P(),
        P(None, None, "tp"),
        P("tp", None),
        P(None, "tp"),
        P("tp"),
        P(None, "tp"),
        P(),
        P(),
        P(None, None, "tp"),
        P("tp", None),
        P(None, "tp"),
        P("tp"),
        P(None, "tp"),
        P(),
        P(),
        P(None, None, "tp"),
        P("tp", None),
        P(None, "tp"),
        P("tp"),
        P(None, "tp"),
        P(),
        P(),
        P("dp", "tp", None),
    )
    return jax.shard_map(
        per_device, mesh=mesh, in_specs=in_specs, out_specs=out_specs, check_vma=False
    )
```

```python
import functools
import math

import jax
import jax.numpy as jnp
from jax import lax
from jax.experimental import pallas as pl
from jax.experimental.pallas import tpu as pltpu
from jax.sharding import PartitionSpec as P

CHN = 96
HDIM = 48
HPAD = 64
HEAD = 384


EPSILON = 1e-05
MOMENTUM_RATE = 0.9
LEARN_RATE = 0.02
AVERAGE_RATE = 0.9
SCALE = HDIM ** (-0.5)
LOG_SCALE = SCALE * math.log2(math.e)
GELU_A = math.sqrt(2.0 / math.pi)
GELU_B = 0.044715
SMALL = 16
BLOCK = 384
ROWS = 128
CHUNKS = 3

bf16 = jnp.bfloat16
f32 = jnp.float32
HBM = pl.BlockSpec(memory_space=pltpu.HBM)
SMEM = pl.BlockSpec(memory_space=pltpu.SMEM)
VMEM = pl.BlockSpec(memory_space=pltpu.VMEM)


def kernel_call(body, outs, inputs, limit, micros, name, in_specs=None, out_specs=None, scratch=(), aliases=None):
    return pl.pallas_call(
        body,
        out_shape=outs,
        in_specs=in_specs or [VMEM] * len(inputs),
        out_specs=out_specs or jax.tree.map(lambda _: VMEM, outs),
        scratch_shapes=list(scratch),
        input_output_aliases=aliases or {},
        compiler_params=pltpu.CompilerParams(vmem_limit_bytes=limit << 20),
        cost_estimate=pl.CostEstimate(flops=int(micros * 1e9), bytes_accessed=0, transcendentals=0),
        name=name,
    )(*inputs)


def struct(rows, columns, dtype):
    return jax.ShapeDtypeStruct((rows, columns), dtype)


def contract(left, right, left_dim, right_dim):
    return lax.dot_general(
        left, right, (((left_dim,), (right_dim,)), ((), ())), preferred_element_type=f32
    )


def row_mean(values):
    return jnp.mean(values, axis=-1, keepdims=True)


def column_sum(values):
    return jnp.sum(values, axis=0, keepdims=True)


def normalise(values):
    centred = values - row_mean(values)
    inverse = lax.rsqrt(row_mean(centred * centred) + EPSILON)
    return centred * inverse, inverse


def aligned(index, size):
    return pl.ds(pl.multiple_of(index * size, size), size)


def forward_body(first, heads, query, key, value, *refs):
    mixed, totals, weights, slots, sems = refs[-5:]

    def out_copy(h):
        slot = lax.rem(h, 2)
        return pltpu.make_async_copy(slots.at[slot], weights.at[h + first], sems.at[slot])

    def head(h, carry):
        @pl.when(h >= 2)
        def _():
            out_copy(h - 2).wait()

        rows = aligned(h, HDIM)
        scores = contract(query[rows], key[rows], 0, 0)
        maximum = jnp.max(scores, axis=1, keepdims=True)
        exponent = jnp.exp2((scores - maximum) * LOG_SCALE).astype(bf16)
        slots[lax.rem(h, 2)] = exponent
        out_copy(h).start()
        summed = contract(value[aligned(h, HPAD)], exponent, 1, 1)
        total = summed[HDIM : HDIM + 1]
        mixed[rows] = (summed[:HDIM] / total).astype(bf16)
        totals[pl.ds(h, 1)] = total
        return carry

    lax.fori_loop(0, heads, head, 0)
    for h in range(max(0, heads - 2), heads):
        out_copy(h).wait()


def attention_forward(query, key, value, weights=None):
    heads = query.shape[0] // HDIM
    first = 0 if weights is None else heads
    rows, length = query.shape[1], key.shape[1]
    return kernel_call(
        functools.partial(forward_body, first, heads),
        [
            struct(heads * HDIM, rows, bf16),
            struct(heads, rows, f32),
            jax.ShapeDtypeStruct((2 * heads, rows, length), bf16),
        ],
        (query, key, value) if weights is None else (query, key, value, weights),
        FORWARD_LIMIT,
        4 * heads,
        "attention_forward",
        in_specs=[VMEM] * 3 if weights is None else [VMEM] * 3 + [HBM],
        aliases={} if weights is None else {3: 2},
        out_specs=[VMEM, VMEM, HBM],
        scratch=[pltpu.VMEM((2, rows, length), bf16), pltpu.SemaphoreType.DMA((2,))],
    )


def backward_body(
    first, base, heads, query, key, value, mixed, grad_mixed, totals, weights,
    grad_query, grad_key, grad_value, slots, sums, scaled_all, sems
):
    def in_copy(h):
        slot = lax.rem(h, 2)
        return pltpu.make_async_copy(weights.at[h + base], slots.at[slot], sems.at[slot])

    in_copy(0).start()
    width = key.shape[1] // CHUNKS

    def head(h, carry):
        @pl.when(h + 1 < heads)
        def _():
            in_copy(h + 1).start()

        rows, here = aligned(h + first, HDIM), aligned(h, HDIM)
        inverse = 1.0 / totals[pl.ds(h + first, 1)]
        grad = grad_mixed[rows].astype(f32)
        delta = column_sum(grad * mixed[rows].astype(f32))
        scaled = (grad * inverse).astype(bf16)
        offset = -delta * inverse
        high = offset.astype(bf16).astype(f32)
        row = lax.broadcasted_iota(jnp.int32, (HPAD - HDIM, offset.shape[1]), 0)
        extra = jnp.where(row == 0, high, jnp.where(row == 1, offset - high, 0.0)).astype(bf16)
        scaled_all[...] = jnp.concatenate([scaled, extra], axis=0)
        sums[...] = jnp.zeros_like(sums)
        in_copy(h).wait()

        def chunk(i, carry):
            part = aligned(i, width)
            grad_weights = contract(scaled_all[...], value[aligned(h + first, HPAD), part], 0, 0)
            kept = slots[lax.rem(h, 2), :, part]
            grad_scores = (kept.astype(f32) * grad_weights).astype(bf16)
            sums[...] += contract(key[rows, part], grad_scores, 1, 1)
            grad_key[here, part] = (contract(query[rows], grad_scores, 1, 0) * SCALE).astype(bf16)
            grad_value[here, part] = contract(scaled_all[:HDIM], kept, 1, 0).astype(bf16)
            return carry

        lax.fori_loop(0, CHUNKS, chunk, 0)
        grad_query[here] = (sums[...] * SCALE).astype(bf16)
        return carry

    lax.fori_loop(0, heads, head, 0)


def attention_backward(first, base, heads, query, key, value, mixed, grad_mixed, totals, weights):
    rows, length = query.shape[1], key.shape[1]
    return kernel_call(
        functools.partial(backward_body, first, base, heads),
        [
            struct(heads * HDIM, rows, bf16),
            struct(heads * HDIM, length, bf16),
            struct(heads * HDIM, length, bf16),
        ],
        (query, key, value, mixed, grad_mixed, totals, weights),
        BACKWARD_LIMIT,
        5.5 * heads,
        "attention_backward",
        in_specs=[VMEM] * 6 + [HBM],
        scratch=[
            pltpu.VMEM((2, rows, length), bf16),
            pltpu.VMEM((HDIM, rows), f32),
            pltpu.VMEM((HPAD, rows), bf16),
            pltpu.SemaphoreType.DMA((2,)),
        ],
    )


def take_body(place, stacked, taken):
    taken[...] = stacked[place[0]]


def take(stacked, place):
    count, rows, columns = stacked.shape
    return kernel_call(
        take_body, struct(rows, columns, stacked.dtype), (place, stacked), 2, 1, "take", in_specs=[SMEM, VMEM]
    )


def pack_body(place, attn, out, up, down, bias, targets, attn_low, sent, goal):
    share, deep = out.shape[0], up.shape[0]
    base = share + 2 * deep
    goal[...] = targets[place[0]]
    attn_low[...] = attn[...].astype(bf16)
    sent[:share] = out[...].astype(bf16)
    sent[share : share + deep] = up[...].astype(bf16)
    sent[share + deep : base] = down[...].astype(bf16)
    high = bias[...].astype(bf16)
    low = (bias[...] - high.astype(f32)).astype(bf16)
    zeros = jnp.zeros((SMALL - 2, bias.shape[1]), bf16)
    sent[base : base + SMALL] = jnp.concatenate([high, low, zeros], axis=0)


def pack(place, attn, out, up, down, bias, targets):
    rows = out.shape[0] + 2 * up.shape[0] + SMALL
    return kernel_call(
        pack_body,
        [struct(attn.shape[0], HEAD, bf16), struct(rows, HEAD, bf16), struct(targets.shape[1], HEAD, bf16)],
        (place, attn, out, up, down, bias, targets),
        8,
        PACK_MICROS,
        "pack",
        in_specs=[SMEM] + [VMEM] * 6,
    )


def weight_rows(left, right):
    share = left.shape[0] // 3
    return jnp.concatenate(
        [block[m * share : (m + 1) * share] for m in range(3) for block in (left, right)], axis=0
    )


def project_into(normed, left, right, query, key, value):
    weights = weight_rows(left[...], right[...])
    size = weights.shape[0] // 3
    rows = query.shape[1]
    query[...] = contract(weights[:size], normed[:rows], 1, 1).astype(bf16)
    both = contract(weights[size:], normed, 1, 1).astype(bf16)
    key[...] = both[:size]
    row = lax.broadcasted_iota(jnp.int32, (HPAD - HDIM, normed.shape[0]), 0)
    ends = jnp.where(row < 2, 1.0, 0.0).astype(bf16)
    for h in range(size // HDIM):
        value[h * HPAD : h * HPAD + HDIM] = both[size + h * HDIM : size + (h + 1) * HDIM]
        value[h * HPAD + HDIM : (h + 1) * HPAD] = ends


def project_near_body(
    place, frames, got, frames_other, got_other, vectors, left, right, query, key, value, first, every
):
    quarter = got.shape[0]
    for j, source in enumerate((frames, got, frames_other, got_other)):
        part = source[place[0]] if j % 2 == 0 else source[...]
        rows = slice(j * quarter, (j + 1) * quarter)
        every[rows] = part
        first[rows] = (normalise(part.astype(f32))[0] * vectors[0:1] + vectors[1:2]).astype(bf16)
    project_into(first[...], left, right, query, key, value)


def projected(rows, length, size):
    return [
        struct(size, rows, bf16),
        struct(size, length, bf16),
        struct(size // HDIM * HPAD, length, bf16),
    ]


def project_near(place, frames, got, frames_other, got_other, vectors, left, right):
    quarter, model = got.shape
    size = 2 * left.shape[0] // 3
    return kernel_call(
        project_near_body,
        projected(2 * quarter, 4 * quarter, size) + [struct(4 * quarter, model, bf16)] * 2,
        (place, frames, got, frames_other, got_other, vectors, left, right),
        16,
        4,
        "project_near",
        in_specs=[SMEM] + [VMEM] * 7,
    )


def project_far_body(first, *refs):
    project_into(first[...], *refs)


def project_far(first, left, right):
    length = first.shape[0]
    size = 2 * left.shape[0] // 3
    return kernel_call(
        project_far_body,
        projected(length // 2, length, size),
        (first, left, right),
        12,
        3,
        "project_far",
    )


def by_rows(function, *values):
    pieces = [
        function(*(v[start : start + ROWS] for v in values)) for start in range(0, values[0].shape[0], ROWS)
    ]
    return [jnp.concatenate(parts, axis=0) for parts in zip(*pieces)]


def middle_body(
    place, attended_near, attended_far, frames, targets, goal_got, keep, vectors, head, *refs
):
    blocks = refs[:4]
    grad_middle_out, grad_near, grad_far, kept_out, sent_out, small_out = refs[4:10]
    second_all, ffn_all, final_all, pred_all, attn_all, hidden_all, pre_all, goal, bias_sums = refs[10:]
    rows = grad_middle_out.shape[0]
    quarter = targets.shape[1]
    deep = head.shape[0]
    share = grad_near.shape[0] // 2
    base = share + 2 * deep
    half = 2 * share
    goal[:quarter] = targets[place[1]]
    goal[quarter:] = goal_got[...]
    gain, shift = vectors[4:5], vectors[5:6]
    scale_one, scale_two = vectors[3:4], vectors[7:8]
    out_low = jnp.concatenate([b[:share] for b in blocks], axis=0)
    head_low = head[...].astype(bf16)
    small_out[...] = jnp.zeros_like(small_out)
    bias_sums[...] = jnp.zeros_like(bias_sums)

    def block_step(step, carry):
        here = aligned(step, BLOCK)

        def add(row, values):
            small_out[row : row + 1] += column_sum(values)

        mixed = contract(attended_near[:, here], out_low[:half], 0, 0) + contract(
            attended_far[:, here], out_low[half:], 0, 0
        )

        def first_norm(mixed, frames):
            biased = mixed + vectors[2:3]
            middle = frames.astype(f32) + scale_one * biased
            normed, inverse = normalise(middle)
            return biased, middle, normed, inverse, (normed * gain + shift).astype(bf16)

        biased_one, middle, normed, inverse, second = by_rows(first_norm, mixed, frames[here])
        second_all[here] = second
        slopes = []
        mixed = None
        for j, block in enumerate(blocks):
            parts = block[base : base + SMALL].astype(f32)
            bias = parts[0:1] + parts[1:2]

            def gelu(pre):
                pre = pre + bias
                square = pre * pre
                tanh = jnp.tanh(pre * (GELU_A + (GELU_A * GELU_B) * square))
                phi = 0.5 + 0.5 * tanh
                curve = (1.0 - tanh * tanh) * (0.5 * GELU_A + (1.5 * GELU_A * GELU_B) * square)
                return (pre * phi).astype(bf16), phi + pre * curve

            hidden, slope = by_rows(gelu, contract(second, block[share : share + deep], 1, 0))
            hidden_all[j, here] = hidden
            slopes.append(slope)
            part = contract(hidden, block[share + deep : base], 1, 1)
            mixed = part if j == 0 else mixed + part

        def second_scale(mixed, middle):
            biased = mixed + vectors[6:7]
            return biased, (middle + scale_two * biased).astype(bf16)

        biased_two, final = by_rows(second_scale, mixed, middle)
        final_all[here] = final

        def error(pred, goal):
            diff = pred + vectors[8:9] - goal.astype(f32)
            smooth = jnp.sqrt(diff * diff + 1.0)
            add(7, keep[...] * (smooth - 1.0) / HEAD)
            grad = (keep[...] * (diff / smooth) / HEAD).astype(bf16)
            add(6, grad.astype(f32))
            return (grad,)

        (grad_pred,) = by_rows(error, contract(final, head_low, 1, 0), goal[here])
        pred_all[here] = grad_pred

        grad_final = contract(grad_pred, head_low, 1, 1)

        def scale_back(grad, biased):
            ffn = grad * scale_two
            add(4, ffn)
            add(5, grad * biased)
            return (ffn.astype(bf16),)

        (ffn_low,) = by_rows(scale_back, grad_final, biased_two)
        ffn_all[here] = ffn_low
        grad_second = None
        for j, block in enumerate(blocks):

            def gelu_back(grad, slope):
                low = (grad * slope).astype(bf16)
                bias_sums[j : j + 1] += column_sum(low.astype(f32))
                return (low,)

            grad = contract(ffn_low, block[share + deep : base], 1, 0)
            (low,) = by_rows(gelu_back, grad, slopes[j])
            pre_all[j, here] = low
            part = contract(low, block[share : share + deep], 1, 1)
            grad_second = part if j == 0 else grad_second + part

        def norm_back(grad, normed, inverse, grad_final, biased):
            add(2, grad * normed)
            add(3, grad)
            scaled = grad * gain
            back = inverse * (scaled - row_mean(scaled) - normed * row_mean(scaled * normed))
            total = grad_final + back
            attn = total * scale_one
            add(0, attn)
            add(1, total * biased)
            return total, attn.astype(bf16)

        grad_middle, attn_low = by_rows(norm_back, grad_second, normed, inverse, grad_final, biased_one)
        grad_middle_out[here] = grad_middle
        attn_all[here] = attn_low
        grad_near[:, here] = contract(out_low[:half], attn_low, 1, 1).astype(bf16)
        grad_far[:, here] = contract(out_low[half:], attn_low, 1, 1).astype(bf16)
        return carry

    lax.fori_loop(0, rows // BLOCK, block_step, 0)

    attn_low = attn_all[...]
    grad_out = jnp.concatenate(
        [contract(attended_near[...], attn_low, 1, 0), contract(attended_far[...], attn_low, 1, 0)], axis=0
    ).astype(bf16)
    for j in range(4):
        target = (kept_out, sent_out)[j % 2]
        start = (j // 2) * base
        target[start : start + share] = grad_out[j * share : (j + 1) * share]
        small_out[pl.ds(8 + lax.bitwise_xor(place[0], j), 1)] = bias_sums[j : j + 1]

    def weight_step(i, carry):
        for k, target in enumerate((kept_out, sent_out)):
            start = pl.multiple_of(i * base + share, SMALL)
            up = contract(second_all[...], pre_all[2 * i + k], 0, 0).astype(bf16)
            down = contract(ffn_all[...], hidden_all[2 * i + k], 0, 0).astype(bf16)
            target[pl.ds(start, deep)] = up
            target[pl.ds(pl.multiple_of(start + deep, SMALL), deep)] = down
        return carry

    lax.fori_loop(0, 2, weight_step, 0)
    grad_head = contract(final_all[...], pred_all[...], 0, 0).astype(bf16)
    column = lax.broadcasted_iota(jnp.int32, (1, HEAD), 1)
    loss = jnp.sum(small_out[7:8], axis=1, keepdims=True)
    small_out[7:8] = jnp.where(column == 0, loss, 0.0)
    core = lax.rem(place[0], 2)
    size = deep // 2
    for target, first in ((kept_out, core == 0), (sent_out, core == 1)):
        target[2 * base : 2 * base + size] = jnp.where(first, grad_head[:size], grad_head[size:])
        target[2 * base + size :] = jnp.zeros((2 * SMALL, HEAD), bf16)


def middle_step(place, attended_near, attended_far, frames, targets, goal_got, keep, vectors, head, blocks):
    rows, model = frames.shape[0] // 2, frames.shape[1]
    base = blocks[0].shape[0] - SMALL
    count = 2 * base + HEAD // 2 + 2 * SMALL
    inputs = (place, attended_near, attended_far, frames, targets, goal_got, keep, vectors, head, *blocks)
    return kernel_call(
        middle_body,
        [
            struct(rows, model, f32),
            struct(*attended_near.shape, bf16),
            struct(*attended_far.shape, bf16),
            struct(count, HEAD, bf16),
            struct(count, HEAD, bf16),
            struct(SMALL, HEAD, f32),
        ],
        inputs,
        MIDDLE_LIMIT,
        20,
        "middle_step",
        in_specs=[SMEM] + [VMEM] * 12,
        scratch=[
            *[pltpu.VMEM((rows, model), bf16)] * 5,
            pltpu.VMEM((4, rows, HEAD), bf16),
            pltpu.VMEM((4, rows, HEAD), bf16),
            pltpu.VMEM((rows, HEAD), bf16),
            pltpu.VMEM((8, HEAD), f32),
        ],
    )


def fold_body(plan, place, left, right, *targets):
    for target, ranges in zip(targets, plan):
        base = 0
        for start, stop, *choice in ranges:
            if choice:
                size = (stop - start) // 2
                source = pl.ds(pl.multiple_of(start + choice[0](place) * size, SMALL), size)
            else:
                size = stop - start
                source = pl.ds(start, size)
            total = left[source].astype(f32) + right[source].astype(f32)
            target[base : base + size] = total.astype(target.dtype)
            base += size


def fold(left, right, plan, place=None, dtype=bf16):
    shapes = [
        struct(sum((r[1] - r[0]) // (2 if len(r) > 2 else 1) for r in ranges), left.shape[1], dtype)
        for ranges in plan
    ]
    if place is None:
        place = jnp.zeros((1,), jnp.int32)
    return kernel_call(
        functools.partial(fold_body, plan),
        shapes,
        (place, left, right),
        6,
        0.3,
        "fold",
        in_specs=[SMEM, VMEM, VMEM],
    )


def join_body(bit, place, kept, got, both):
    size = kept.shape[0]
    both[pl.ds(pl.multiple_of(bit(place) * size, SMALL), size)] = kept[...]
    both[pl.ds(pl.multiple_of((1 - bit(place)) * size, SMALL), size)] = got[...]


def join(kept, got, bit, place):
    return kernel_call(
        functools.partial(join_body, bit),
        struct(2 * kept.shape[0], kept.shape[1], kept.dtype),
        (place, kept, got),
        6,
        0.3,
        "join",
        in_specs=[SMEM, VMEM, VMEM],
    )


def gather_rows(parts):
    return jnp.concatenate([p[...] for p in parts], axis=0)


def weight_grads(grads, first, kept, sent, base=0):
    queries, keys, values = grads
    rows = queries[0].shape[1]
    query = contract(gather_rows(queries), first[:rows], 1, 0)
    both = contract(gather_rows(keys + values), first[...], 1, 0)
    share = query.shape[0] // 2
    for m in range(3):
        for j, target in enumerate((kept, sent)):
            start = (max(m - 1, 0) * 2 + j) * share
            part = (query if m == 0 else both)[start : start + share]
            target[m * share : (m + 1) * share] = part.astype(bf16)


def far_grads_body(calls, first, *refs):
    grads = [refs[k * calls : (k + 1) * calls] for k in range(3)]
    weight_grads(grads, first[...], *refs[3 * calls :])


def far_grads(grads, first):
    queries, keys, values = zip(*grads)
    count = 3 * sum(q.shape[0] for q in queries) // 2
    return kernel_call(
        functools.partial(far_grads_body, len(grads)),
        [struct(count, HEAD, bf16)] * 2,
        (first, *queries, *keys, *values),
        12,
        4,
        "far_grads",
    )


def post_body(calls, near, *refs):
    queries, keys, values = (refs[k * calls : (k + 1) * calls] for k in range(3))
    first, frames, vectors, small_in = refs[3 * calls : 3 * calls + 4]
    blocks = refs[3 * calls + 4 : 3 * calls + 8]
    mine, other, kept, sent, small = refs[3 * calls + 8 :]
    share = blocks[0].shape[0] // 3
    rows = mine.shape[0]

    def rows_of(m):
        return jnp.concatenate([b[m * share : (m + 1) * share] for b in blocks], axis=0)

    weight_grads((queries[:near], keys[:near], values[:near]), first[...], kept, sent)
    both = jnp.concatenate([rows_of(1), rows_of(2)], axis=0)
    query_rows = rows_of(0)
    small[...] = small_in[...]

    def part(step, carry):
        here = aligned(step, BLOCK)
        there = pl.ds(pl.multiple_of(rows + step * BLOCK, BLOCK), BLOCK)

        def pulled(parts, columns, weights):
            return contract(jnp.concatenate([p[:, columns] for p in parts], axis=0), weights, 0, 0)

        def ends(total, place):
            normed = normalise(frames[place].astype(f32))[0]
            small[12:13] += column_sum(total * normed)
            small[13:14] += column_sum(total)

        total = pulled(keys + values, here, both) + pulled(queries, here, query_rows)
        mine[here] = total
        ends(total, here)
        rest = pulled(keys + values, there, both)
        other[here] = rest.astype(bf16)
        ends(rest, there)
        return carry

    lax.fori_loop(0, rows // BLOCK, part, 0)


def post_step(grads, first, frames, vectors, small, blocks):
    length, model = first.shape
    rows = length // 2
    queries, keys, values = zip(*grads)
    payload = struct(blocks[0].shape[0], model, bf16)
    return kernel_call(
        functools.partial(post_body, len(grads), 2),
        [struct(rows, model, f32), struct(rows, model, bf16), payload, payload, struct(*small.shape, f32)],
        (*queries, *keys, *values, first, frames, vectors, small, *blocks),
        POST_LIMIT,
        8,
        "post_step",
    )


def finish_body(mine, got, frames, vectors, grad_middle, own, returned):
    quarter = own.shape[0]
    size = quarter // 3

    def part(step, carry):
        for target, base in ((own, 0), (returned, quarter)):
            there = aligned(step, size)
            here = pl.ds(pl.multiple_of(base + step * size, size), size)
            grad = mine[here] + got[here].astype(f32)
            normed, inverse = normalise(frames[here].astype(f32))
            scaled = grad * vectors[0:1]
            back = inverse * (scaled - row_mean(scaled) - normed * row_mean(scaled * normed))
            target[there] = (grad_middle[here] + back).astype(target.dtype)
        return carry

    lax.fori_loop(0, 3, part, 0)


def finish(mine, got, frames, vectors, grad_middle):
    rows, model = mine.shape
    return kernel_call(
        finish_body,
        [struct(rows // 2, model, f32), struct(rows // 2, model, bf16)],
        (mine, got, frames, vectors, grad_middle),
        16,
        3,
        "finish",
    )


def update(weight, moment, average, grad):
    moment_new = MOMENTUM_RATE * moment + grad
    weight_new = weight - LEARN_RATE * (grad + MOMENTUM_RATE * moment_new)
    average_new = AVERAGE_RATE * average + (1.0 - AVERAGE_RATE) * weight_new
    return (weight_new, moment_new, average_new)


CORE_PAIRS = [(0, 1), (1, 0), (2, 3), (3, 2)]
CHIP_PAIRS = [(0, 2), (2, 0), (1, 3), (3, 1)]
FORWARD_LIMIT = 28
BACKWARD_LIMIT = 28
MIDDLE_LIMIT = 30
POST_LIMIT = 20
PACK_MICROS = 3


def swap_core(values):
    return lax.ppermute(values, "tp", CORE_PAIRS)


def swap_chip(values):
    return lax.ppermute(values, "tp", CHIP_PAIRS)


def swap_dp(values, step, size):
    return lax.ppermute(values, "dp", [(i, i ^ step) for i in range(size)])


def pick(stacked, place):
    return lax.dynamic_index_in_dim(stacked, place, 0, False)


def tie(value, *others):
    return lax.optimization_barrier((value, *others))[0]


def per_device(
    frames,
    targets,
    presence,
    order,
    attn_proj,
    out_proj,
    up_proj,
    up_bias,
    down_proj,
    head_proj,
    vectors,
    momentum_attn,
    momentum_out,
    momentum_up,
    momentum_bias,
    momentum_down,
    momentum_head,
    momentum_vectors,
    average_attn,
    average_out,
    average_up,
    average_bias,
    average_down,
    average_head,
    average_vectors,
):
    size = lax.axis_size("dp")
    place = lax.axis_index("tp")
    chip, core = place // 2, place % 2
    share, deep = out_proj.shape[0], up_proj.shape[0]
    got = swap_chip(take(frames, (1 - chip).reshape(1)))
    frames_other = swap_core(frames)
    attn_own, sent, goal = pack(
        order[0, 1 - chip].reshape(1),
        jnp.swapaxes(attn_proj, 1, 2).reshape(3 * share, HEAD),
        out_proj,
        up_proj,
        down_proj,
        up_bias[None],
        targets,
    )
    attn_core = swap_core(attn_own)
    sent_core = swap_core(sent)
    got_other = swap_core(tie(got, attn_own))
    attn_chip = swap_chip(tie(attn_own, got))
    query, key, value, first, every = project_near(
        chip.reshape(1), frames, got, frames_other, got_other, vectors, attn_own, attn_core
    )
    sent_chip = swap_chip(tie(sent, first))
    near = (query, key, value)
    near_out = attention_forward(*near)
    attn_both = swap_core(tie(attn_chip, first))
    far = project_far(tie(first, near_out[0]), attn_chip, attn_both)
    sent_both = swap_core(tie(sent_chip, far[0]))
    goal_got = swap_chip(tie(goal, far[0]))
    far_out = attention_forward(*far, near_out[2])
    keep = jnp.repeat(pick(presence, chip).astype(f32), CHN)[None, :]
    where = jnp.stack([place, order[0, chip]])
    grad_middle, grad_near, grad_far, kept, sent, small = middle_step(
        where, near_out[0], far_out[0], every, targets, goal_got, keep, vectors, head_proj,
        (sent, sent_core, sent_chip, sent_both),
    )

    inputs = ((*near, near_out[0], grad_near, near_out[1], far_out[2]), (*far, far_out[0], grad_far, *far_out[1:]))
    here = near[0].shape[0] // HDIM

    def backward(part, first_head, heads, *after):
        query, *others = inputs[part]
        return attention_backward(first_head, part * here + first_head, heads, tie(query, *after), *others)

    block = share + 2 * deep
    half = HEAD // 2
    full = block + half + 2 * SMALL
    spot = lax.axis_index("dp").reshape(1)
    bits = [lambda p: p[0] % 2, lambda p: p[0] // 2 % 2]
    others = [lambda p: 1 - p[0] % 2, lambda p: 1 - p[0] // 2 % 2]
    steps = [1 << k for k in range(size.bit_length() - 1)]
    last_rows = (2 * block, full + block)
    rows = 3 * share

    got_core = swap_core(sent)
    kept, sent = fold(
        kept, got_core, [[(0, block), last_rows], [(block, 2 * block), last_rows]]
    )
    got_chip = swap_chip(sent)
    far_all = backward(1, 0, here, sent)
    kept, sent = fold(
        kept, tie(got_chip, far_all[0]), [[(0, full, bits[0])], [(0, full, others[0])]], spot
    )
    got_y = swap_dp(sent, 1, size)
    far_kept, far_sent = far_grads([far_all], tie(first, sent))
    got_far = swap_core(far_sent)
    near_one = backward(0, 0, here // 2, sent, far_sent)
    (far_kept,) = fold(far_kept, tie(got_far, near_one[0]), [[(0, rows)]])
    got_far = swap_chip(far_kept)
    kept, sent = fold(
        kept, tie(got_y, near_one[0]), [[(0, full // 2, bits[1])], [(0, full // 2, others[1])]], spot
    )
    got_z = swap_dp(sent, 2, size)
    near_two = backward(0, here // 2, here // 2, sent, far_kept)
    (kept,) = fold(kept, tie(got_z, near_two[0]), [[(0, full // 4)]])
    got_step = swap_dp(kept, steps[2], size)
    mine, other, near_kept, near_sent, small = post_step(
        [near_one, near_two, far_all],
        tie(first, kept, got_far),
        every,
        vectors,
        small,
        (attn_own, attn_core, attn_chip, attn_both),
    )
    got_near = swap_core(near_sent)
    got_small = swap_core(small)
    other_rows = swap_core(other)
    (near_kept,) = fold(near_kept, got_far, [[(0, rows)]], dtype=f32)
    (attn_kept,) = fold(near_kept, got_near, [[(0, rows)]])
    got_attn = swap_dp(attn_kept, 1, size)
    (small,) = fold(small, tie(got_small, attn_kept), [[(0, SMALL)]], dtype=f32)
    got_small = swap_chip(small)
    own_rows, returned = finish(mine, other_rows, every, vectors, tie(grad_middle, attn_kept, small))
    (small,) = fold(small, tie(got_small, own_rows), [[(0, SMALL)]], dtype=f32)
    returned = swap_chip(tie(returned, small))
    def settle(kept, got_kept, returned):
        kept = join(kept, got_kept, bits[0], spot)
        returned = returned.astype(f32)
        grad_frames = jnp.where(
            chip == 0, jnp.stack([own_rows, returned]), jnp.stack([returned, own_rows])
        )
        kept = kept.astype(f32)
        grad_out = kept[:share]
        grad_up = kept[share : share + deep]
        grad_down = kept[share + deep : block]
        head_mine = kept[block : block + half]
        head_other = swap_core(head_mine.astype(bf16)).astype(f32)
        grad_head = jnp.where(
            core == 0,
            jnp.concatenate([head_mine, head_other], axis=0),
            jnp.concatenate([head_other, head_mine], axis=0),
        )
        second_set = update(out_proj, momentum_out, average_out, grad_out)
        third_set = update(up_proj, momentum_up, average_up, grad_up)
        fifth_set = update(down_proj, momentum_down, average_down, grad_down)
        sixth_set = update(head_proj, momentum_head, average_head, grad_head)
        return grad_frames, *second_set, *third_set, *fifth_set, *sixth_set

    for step in steps:
        got_small = swap_dp(small, step, size)
        if step == steps[-1]:
            last = settle(kept, got_kept, returned)
            got_attn = tie(got_attn, last[0])
        (attn_kept,) = fold(
            attn_kept, tie(got_attn, small), [[(0, rows)]], dtype=f32 if step == steps[-1] else bf16
        )
        if step < steps[-1]:
            got_attn = swap_dp(attn_kept, 2 * step, size)
        if step == 2:
            kept = join(kept, tie(got_kept, attn_kept), bits[1], spot)
            got_kept = swap_dp(kept, 1, size)
            got_small = tie(got_small, kept)
        (small,) = fold(small, tie(got_small, attn_kept), [[(0, SMALL)]], dtype=f32)
        if step == 1:
            for high in steps[2:]:
                got_step = tie(got_step, small) if high == steps[2] else swap_dp(kept, high, size)
                (kept,) = fold(kept, got_step, [[(0, full // 4)]])
            got_kept = swap_dp(kept, 2, size)
        elif step == 2:
            returned = tie(returned, attn_kept)
    grad_frames, *sets = last
    second_set, third_set, fifth_set, sixth_set = (sets[k : k + 3] for k in range(0, 12, 3))
    grad_attn_proj = jnp.swapaxes(attn_kept.reshape(3, share, HEAD), 1, 2)
    loss = small[7, 0]
    grad_up_bias = pick(small[8:12], place)
    grad_vectors = jnp.concatenate([small[12:14], small[:7]], axis=0)
    first_set = update(attn_proj, momentum_attn, average_attn, grad_attn_proj)
    fourth_set = update(up_bias, momentum_bias, average_bias, grad_up_bias)
    seventh_set = update(vectors, momentum_vectors, average_vectors, grad_vectors)
    return (
        loss,
        first_set[0],
        second_set[0],
        third_set[0],
        fourth_set[0],
        fifth_set[0],
        sixth_set[0],
        seventh_set[0],
        first_set[1],
        second_set[1],
        third_set[1],
        fourth_set[1],
        fifth_set[1],
        sixth_set[1],
        seventh_set[1],
        first_set[2],
        second_set[2],
        third_set[2],
        fourth_set[2],
        fifth_set[2],
        sixth_set[2],
        seventh_set[2],
        grad_frames,
    )


def solution(mesh):
    in_specs = (
        P("dp", "tp", None),
        P("dp", "tp", None),
        P("dp", None),
        P("dp", None),
        P(None, None, "tp"),
        P("tp", None),
        P(None, "tp"),
        P("tp"),
        P(None, "tp"),
        P(),
        P(),
        P(None, None, "tp"),
        P("tp", None),
        P(None, "tp"),
        P("tp"),
        P(None, "tp"),
        P(),
        P(),
        P(None, None, "tp"),
        P("tp", None),
        P(None, "tp"),
        P("tp"),
        P(None, "tp"),
        P(),
        P(),
    )
    out_specs = (
        P(),
        P(None, None, "tp"),
        P("tp", None),
        P(None, "tp"),
        P("tp"),
        P(None, "tp"),
        P(),
        P(),
        P(None, None, "tp"),
        P("tp", None),
        P(None, "tp"),
        P("tp"),
        P(None, "tp"),
        P(),
        P(),
        P(None, None, "tp"),
        P("tp", None),
        P(None, "tp"),
        P("tp"),
        P(None, "tp"),
        P(),
        P(),
        P("dp", "tp", None),
    )
    return jax.shard_map(
        per_device, mesh=mesh, in_specs=in_specs, out_specs=out_specs, check_vma=False
    )
```
